32 devices in a mesh: outer: 4 (over y, x), inner: 8 (over z, core).
Axes of the slice: x: 2, y: 2, z: 4, core: 2. Of those that a mesh axis runs over, the one named last changes fastest.
Arguments:
- queries: bfloat16 [8192, 512], P(('outer', 'inner')), may hold values from -56 to 56
- keys: bfloat16 [8192, 512], P(('outer', 'inner')), may hold values from -48 to 48
- values: bfloat16 [8192, 512], P(('outer', 'inner')), may hold values from -6 to 6
- out_weight: bfloat16 [512, 768], replicated, may hold values from -0.25 to 0.25
- slide_lengths: int32 [16], replicated, may hold values from 1 to 6144, 8192 in all
Outputs:
- mixed_output: bfloat16 [8192, 768], P(('outer', 'inner'))
The draws below stay inside these ranges and needn't reach their ends.
Inputs may be any that keep to these rules, and one draw needn't show every extreme that they name: `slide_lengths`: the lengths sum to 8192.
All inputs are finite; a program needn't handle non-finite values.
Results may differ from the reference program's by a relative error of at most 0.0052.
Values may be sent and summed in bfloat16 or wider, within the bound.
No kernel may reach another device: no remote copies, remote signals or barrier semaphores. Data moves between devices by JAX's collectives and lax.ppermute only.
A program may use at most 64 MiB of HBM per device.

```python
import math
import jax
import jax.numpy as jnp
import numpy as np
from jax import lax

D = 768
HEADS = 8
HEAD_DIM = 64
SPARSE = 1024
SLIDES = 16
HD = 512
TOKENS = 8192
MID_RATE = 2
TOP_RATE = 8


def draw_pair(key):
    seeds = jax.random.split(jax.random.fold_in(key, 4242), 2)
    width = HEADS * HEAD_DIM
    query_matrix = 3.0 * jax.random.truncated_normal(seeds[0], -6.0, 6.0, (TOKENS, width), jnp.float32)
    keys_matrix = jax.random.truncated_normal(seeds[1], -6.0, 6.0, (TOKENS, width), jnp.float32)
    return (query_matrix, keys_matrix)


def draw_queries(key, part):
    return draw_pair(key)[0].astype(jnp.bfloat16)


def draw_keys(key, part):
    return draw_pair(key)[1].astype(jnp.bfloat16)


def block_levels(own_key, extent, cuts, low, top_value):
    factor_of = 1.0
    for position, parts in cuts:
        draws = jax.random.uniform(jax.random.fold_in(jax.random.fold_in(own_key, 6), position), (parts,), jnp.float32, low / len(cuts), top_value / len(cuts))
        factor_of = factor_of * jnp.repeat(jnp.exp(draws), extent[position] // parts).reshape((-1,) + (1,) * (len(extent) - 1 - position))
    return factor_of


def profile(count, total, reach, skew):
    loads = [(1 << 20) // math.isqrt(rank ** skew) + 1 for rank in range(2, count + 1)]
    surplus, holding = total - reach - (count - 1), [1] * (count - 1)
    while surplus > 0:
        movable = [i for i in range(count - 1) if holding[i] < reach]
        whole, remaining = sum([loads[i] for i in movable]), surplus
        for i in movable:
            addition = min(reach - holding[i], max(1, remaining * loads[i] // whole), surplus)
            holding[i] = holding[i] + addition
            surplus = surplus - addition
    return np.array([reach] + holding)


def ragged(own_key, number_of, total, limit, skew):
    if number_of == 2:
        one = jax.random.randint(own_key, (), max(1, total - limit), min(limit, total - 1) + 1)
        return jnp.stack([one, total - one])
    lengths = jnp.asarray(profile(number_of, total, limit, skew), jnp.int32)
    twos = (number_of - 1) // 2
    giver, receiver = lengths[1:1 + 2 * twos:2], lengths[2:2 + 2 * twos:2]
    slack = jnp.minimum(giver - 1, limit - receiver)
    moved = jax.random.randint(jax.random.fold_in(own_key, 1), (twos,), 0, 1 << 20) % (slack + 1)
    lengths = lengths.at[1:1 + 2 * twos:2].set(giver - moved).at[2:2 + 2 * twos:2].set(receiver + moved)
    return lengths[jax.random.permutation(jax.random.fold_in(own_key, 2), number_of)]


def scatter_about(own_key, dims, scale, bound, cuts=(), kind=jnp.bfloat16):
    drawn = scale * jax.random.normal(own_key, dims, jnp.float32)
    if cuts:
        drawn = drawn * block_levels(own_key, dims, cuts, -0.22, 0.18)
    return jnp.clip(drawn, -bound, bound).astype(kind)


def setup_inputs(seed: int = 0) -> dict:
    streams_of = jax.random.split(jax.random.key(seed), 6)
    queries = draw_queries(jax.random.fold_in(streams_of[5], 71), 0)
    keys = draw_keys(jax.random.fold_in(streams_of[5], 71), 0)
    values = scatter_about(streams_of[2], (TOKENS, HD), 1.0, 6.0, ((0, 32),))
    out_weight = scatter_about(streams_of[3], (HD, D), HD ** -0.5, 0.25)
    slide_lengths = ragged(streams_of[4], SLIDES, TOKENS, 3 * TOKENS // 4, 2).astype(jnp.int32)
    return dict(queries=queries, keys=keys, values=values, out_weight=out_weight, slide_lengths=slide_lengths)


masked_score = -1e30


def slide_index(positions, slide_ends):
    return jnp.sum((positions[:, None] >= slide_ends[None, :]).astype(jnp.int32), axis=1).astype(jnp.int32)


def segment_attention(query_rows, key_rows, value_rows, query_slides, key_slides):
    scores = jnp.dot(query_rows, key_rows.T, preferred_element_type=jnp.float32) * (HEAD_DIM ** -0.5)
    scores = jnp.where(query_slides[:, None] == key_slides[None, :], scores, masked_score)
    row_max = jnp.max(scores, axis=1, keepdims=True)
    expos = jnp.exp(scores - row_max)
    totals = jnp.sum(expos, axis=1, keepdims=True)
    probs = expos.astype(jnp.bfloat16)
    branch = jnp.dot(probs, value_rows, preferred_element_type=jnp.float32) / totals
    return branch, row_max[:, 0] + jnp.log(totals[:, 0])


def mix_levels(first, second, third):
    largest = jnp.maximum(jnp.maximum(first[1], second[1]), third[1])
    weighted = jnp.zeros_like(first[0])
    weight_sum = jnp.zeros_like(first[1])
    for branch, branch_lse in (first, second, third):
        factor = jnp.exp(branch_lse - largest)
        weighted = weighted + factor[:, None] * branch
        weight_sum = weight_sum + factor
    return weighted / weight_sum[:, None]


def level_branch(queries, keys, values, slides, step_rate, head_index):
    offset = head_index % step_rate
    first_column = head_index * HEAD_DIM

    def select_head(matrix):
        grouped = matrix[:, first_column:first_column + HEAD_DIM].reshape(TOKENS // step_rate, step_rate, HEAD_DIM)
        return grouped[:, offset, :].reshape(-1, SPARSE, HEAD_DIM)

    picked_slides = slides.reshape(TOKENS // step_rate, step_rate)[:, offset].reshape(-1, SPARSE)

    def one_segment(pieces):
        return segment_attention(pieces[0], pieces[1], pieces[2], pieces[3], pieces[3])

    branch, branch_lse = lax.map(one_segment, (select_head(queries), select_head(keys), select_head(values), picked_slides))
    full_branch = jnp.zeros((TOKENS // step_rate, step_rate, HEAD_DIM), jnp.float32)
    full_branch = full_branch.at[:, offset, :].set(branch.reshape(-1, HEAD_DIM)).reshape(TOKENS, HEAD_DIM)
    full_lse = jnp.full((TOKENS // step_rate, step_rate), masked_score, jnp.float32)
    full_lse = full_lse.at[:, offset].set(branch_lse.reshape(-1)).reshape(TOKENS)
    return full_branch, full_lse


def reference(queries, keys, values, out_weight, slide_lengths):
    slide_ends = jnp.cumsum(slide_lengths).astype(jnp.int32)
    slides = slide_index(jnp.arange(TOKENS, dtype=jnp.int32), slide_ends)
    head_outputs = []
    for head_index in range(HEADS):
        levels = [level_branch(queries, keys, values, slides, step_rate, head_index) for step_rate in (1, MID_RATE, TOP_RATE)]
        head_outputs.append(mix_levels(levels[0], levels[1], levels[2]))
    attention = jnp.concatenate(head_outputs, axis=1).astype(jnp.bfloat16)
    return jnp.dot(attention, out_weight, preferred_element_type=jnp.float32).astype(jnp.bfloat16)
```

```python
import functools

import jax
import jax.numpy as jnp
from jax import lax
from jax.experimental import pallas as pl
from jax.experimental.pallas import tpu as pltpu
from jax.sharding import PartitionSpec as P

HEADS = 8
HEAD_DIM = 64
SPARSE = 1024
LANES = 128
FAR = 1 << 30
BARRED = -(2.0**100)
F32 = jnp.float32
BF16 = jnp.bfloat16


def exchange(block, axis, distance):
    count = lax.axis_size(axis)
    return lax.ppermute(block, axis, [(i, i ^ distance) for i in range(count)])


def shift_of(value):
    return value.bit_length() - 1


class Plan:
    def __init__(self, rows, inner, outer):
        self.rows = rows
        self.inner = inner
        self.outer = outer
        self.mid = rows * inner // SPARSE
        self.top = self.mid * outer
        self.group = SPARSE // rows
        self.mid_rows = rows // self.mid
        self.top_rows = rows // self.top
        self.top_tile = max(16, self.top_rows)
        assert HEADS == 2 * self.group and 2 * HEAD_DIM == LANES

    def me(self):
        return lax.axis_index("outer") * self.inner + lax.axis_index("inner")

    def pair(self):
        return lax.axis_index("inner") & (self.group - 1)

    def source_row(self, k):
        a = k >> shift_of(self.mid_rows)
        c = (k & (self.mid_rows - 1)) >> shift_of(self.top_rows)
        b = k & (self.top_rows - 1)
        return self.top * b + self.mid * c + a


def dot(a, b, dims):
    return lax.dot_general(a, b, (dims, ((), ())), preferred_element_type=F32)


def pick(wrapped, head, rows):
    return jnp.where(wrapped == ((rows - head) & (rows - 1)), 1.0, 0.0).astype(BF16)


def pack_kernel(plan, q_ref, k_ref, v_ref, *outs):
    rows, group = plan.rows, plan.group
    mains, mids = outs[:group], outs[group:]
    k = lax.broadcasted_iota(jnp.int32, (rows, rows), 0)
    i = lax.broadcasted_iota(jnp.int32, (rows, rows), 1)
    wrapped = (plan.source_row(k) - i) & (rows - 1)
    first = lax.broadcasted_iota(jnp.int32, (rows, 3 * LANES), 1) % LANES < HEAD_DIM
    scale = jnp.where(
        lax.broadcasted_iota(jnp.int32, (rows, 3 * LANES), 1) < LANES, HEAD_DIM**-0.5, 1.0
    )
    for x in range(group):
        pair = plan.pair() ^ x
        columns = pl.ds(pl.multiple_of(pair * LANES, LANES), LANES)
        block = jnp.concatenate([q_ref[:, columns], k_ref[:, columns], v_ref[:, columns]], axis=1)
        one = dot(pick(wrapped, 2 * pair, rows), block, ((1,), (0,)))
        two = dot(pick(wrapped, 2 * pair + 1, rows), block, ((1,), (0,)))
        packed = (jnp.where(first, one, two) * scale).astype(BF16)
        mains[x][...] = packed
        mids[x][...] = packed[: plan.mid_rows, LANES:]


def features(plan, table_ref, t, base, slot_shift, count, kind):
    r = lax.broadcasted_iota(jnp.int32, (count, LANES), 0)
    lane = lax.broadcasted_iota(jnp.int32, (count, LANES), 1)
    head = 2 * plan.pair() + t
    source = plan.me() ^ (base + (r >> slot_shift))
    k = r & ((1 << slot_shift) - 1)
    position = source * plan.rows + ((plan.source_row(k) + head) & (plan.rows - 1))
    starts = table_ref[2 * t : 2 * t + 1, :]
    ends = table_ref[2 * t + 1 : 2 * t + 2, :]
    inside = (position >= starts) & (position < ends)
    own = (lane < HEAD_DIM) if t == 0 else (lane >= HEAD_DIM)
    return inside, own


def as_query(block, inside, own):
    return jnp.where(own, block.astype(F32), jnp.where(inside, BARRED, 0.0)).astype(BF16)


def as_key(block, inside, own):
    return jnp.where(own, block.astype(F32), jnp.where(inside, 0.0, 1.0)).astype(BF16)


def as_value(block, own):
    return jnp.where(own, block.astype(F32), 1.0)


def row_iota(count):
    return lax.broadcasted_iota(jnp.int32, (count, LANES), 0)


def share(total):
    return total / pltpu.roll(total, HEAD_DIM, axis=1)


def local_kernel(plan, table_ref, *refs):
    rows, group, mid_rows, tile = plan.rows, plan.group, plan.mid_rows, plan.top_tile
    mains, refs = refs[:group], refs[group:]
    rest, (sums_one, sums_two, maxima) = refs[:group], refs[group : group + 3]
    q_s, k_s, v_s, v2_s, vt_s = refs[group + 3 :]
    row = row_iota(rows)
    for t in range(2):
        for x in range(group):
            here = pl.ds(x * rows, rows)
            inside, own = features(plan, table_ref, t, x, shift_of(rows), rows, None)
            q_s[t, here, :] = as_query(mains[x][:, :LANES], inside, own)
            k_s[t, here, :] = as_key(mains[x][:, LANES : 2 * LANES], inside, own)
            value = as_value(mains[x][:, 2 * LANES :], own)
            v_s[t, here, :] = value.astype(BF16)
            v2_s[t, here, :] = jnp.where(row < mid_rows, 2.0 * value, value).astype(BF16)
            vt_s[t, here, :] = jnp.where(row < plan.top_rows, value, 0.0).astype(BF16)
    for x in range(group):
        here = pl.ds(x * rows, rows)
        out = []
        big = []
        for t in range(2):
            scores = dot(q_s[t, here, :], k_s[t], ((1,), (1,)))
            largest = jnp.max(scores, axis=1, keepdims=True)
            probs = jnp.exp(scores - largest).astype(BF16)
            mid_sum = dot(probs[:mid_rows], v2_s[t], ((1,), (0,)))
            top_sum = dot(probs[:tile], vt_s[t], ((1,), (0,)))
            rest_sum = dot(probs[mid_rows:], v_s[t], ((1,), (0,)))
            sums = (sums_one, sums_two)[t]
            sums[pl.ds(x * mid_rows, mid_rows), :] = mid_sum
            sums[pl.ds(x * mid_rows, tile), :] += jnp.where(
                row_iota(tile) < plan.top_rows, top_sum, 0.0
            )
            out.append(share(rest_sum))
            big.append(jnp.broadcast_to(largest[:mid_rows], (mid_rows, LANES)))
        lane = lax.broadcasted_iota(jnp.int32, (rows - mid_rows, LANES), 1)
        rest[x][...] = jnp.where(lane < HEAD_DIM, out[0], out[1]).astype(BF16)
        lane = lax.broadcasted_iota(jnp.int32, (mid_rows, LANES), 1)
        maxima[pl.ds(x * mid_rows, mid_rows), :] = jnp.where(lane < HEAD_DIM, big[0], big[1])


def upper_kernel(plan, table_ref, sums_one, sums_two, maxima, *refs):
    group, mid_rows, tile = plan.group, plan.mid_rows, plan.top_tile
    mains, refs = refs[:group], refs[group:]
    mids, refs = refs[: plan.inner - group], refs[plan.inner - group :]
    tops, outs = refs[: plan.outer - 1], refs[plan.outer - 1 :]
    count = group * mid_rows
    lane = lax.broadcasted_iota(jnp.int32, (count, LANES), 1)
    row = row_iota(count) & (mid_rows - 1)
    queries = jnp.concatenate([main[...] for main in mains], axis=0)
    mid_kv = jnp.concatenate([mid[...] for mid in mids], axis=0)
    top_kv = jnp.concatenate([top[...] for top in tops], axis=0)
    results = []
    for t in range(2):
        inside, own = features(plan, table_ref, t, 0, shift_of(mid_rows), count, None)
        q = as_query(queries, inside, own)
        n_mid = mid_kv.shape[0]
        inside, own = features(plan, table_ref, t, group, shift_of(mid_rows), n_mid, None)
        key = as_key(mid_kv[:, :LANES], inside, own)
        value = as_value(mid_kv[:, LANES:], own)
        key_row = row_iota(n_mid) & (mid_rows - 1)
        top_value = jnp.where(key_row < plan.top_rows, value, 0.0).astype(BF16)
        sums = (sums_one, sums_two)[t][...]
        old = maxima[:, t * HEAD_DIM : t * HEAD_DIM + 1]
        scores = dot(q, key, ((1,), (1,)))
        new = jnp.maximum(old, jnp.max(scores, axis=1, keepdims=True))
        probs = jnp.exp(scores - new).astype(BF16)
        sums = sums * jnp.exp(old - new) + dot(probs, value.astype(BF16), ((1,), (0,)))

        def leading(array):
            return jnp.concatenate(
                [array[x * mid_rows : x * mid_rows + tile] for x in range(group)], axis=0
            )

        top_count = group * tile
        is_top = (row_iota(top_count) & (tile - 1)) < plan.top_rows
        extra = dot(leading(probs), top_value, ((1,), (0,)))
        n_top = top_kv.shape[0]
        inside, own = features(plan, table_ref, t, plan.inner, shift_of(plan.top_rows), n_top, None)
        key = as_key(top_kv[:, :LANES], inside, own)
        value = as_value(top_kv[:, LANES:], own).astype(BF16)
        scores = dot(leading(q), key, ((1,), (1,)))
        old = leading(new)
        new = jnp.maximum(old, jnp.max(scores, axis=1, keepdims=True))
        probs = jnp.exp(scores - new).astype(BF16)
        head = leading(sums)
        lead = (head + extra) * jnp.exp(old - new) + dot(probs, value, ((1,), (0,)))
        lead = jnp.where(is_top, lead, head)
        parts = []
        for x in range(group):
            parts.append(lead[x * tile : (x + 1) * tile])
            if tile < mid_rows:
                parts.append(sums[x * mid_rows + tile : (x + 1) * mid_rows])
        results.append(share(jnp.concatenate(parts, axis=0)))
    both = jnp.where(lane < HEAD_DIM, results[0], results[1]).astype(BF16)
    for x in range(group):
        outs[x][...] = both[x * mid_rows : (x + 1) * mid_rows]


def project_kernel(plan, weight_ref, *refs):
    rows, group = plan.rows, plan.group
    mids, rests, (out_ref, flat) = refs[:group], refs[group : 2 * group], refs[2 * group :]
    i = lax.broadcasted_iota(jnp.int32, (rows, rows), 0)
    k = lax.broadcasted_iota(jnp.int32, (rows, rows), 1)
    wrapped = (plan.source_row(k) - i) & (rows - 1)
    lane = lax.broadcasted_iota(jnp.int32, (rows, LANES), 1)
    for x in range(group):
        pair = plan.pair() ^ x
        block = jnp.concatenate([mids[x][...], rests[x][...]], axis=0)
        one = dot(pick(wrapped, 2 * pair, rows), block, ((1,), (0,)))
        two = dot(pick(wrapped, 2 * pair + 1, rows), block, ((1,), (0,)))
        columns = pl.ds(pl.multiple_of(pair * LANES, LANES), LANES)
        flat[:, columns] = jnp.where(lane < HEAD_DIM, one, two).astype(BF16)
    out_ref[...] = dot(flat[...], weight_ref[...], ((1,), (0,))).astype(BF16)


def slide_table(slide_lengths):
    slides = slide_lengths.shape[0]
    lane = jnp.arange(LANES, dtype=jnp.int32)
    index = jnp.arange(slides, dtype=jnp.int32)
    table = []
    for t in range(2):
        slide = lane - (HEAD_DIM if t == 0 else 0)
        valid = (slide >= 0) & (slide < slides)
        for bound in range(2):
            before = index[None, :] < (slide + bound)[:, None]
            total = jnp.sum(jnp.where(before, slide_lengths[None, :], 0), axis=1)
            table.append(jnp.where(valid, total, FAR))
    return jnp.stack(table + table, axis=0).astype(jnp.int32)


def shards(queries, keys, values, out_weight, slide_lengths):
    plan = Plan(queries.shape[0], lax.axis_size("inner"), lax.axis_size("outer"))
    rows, group, mid_rows = plan.rows, plan.group, plan.mid_rows
    table = slide_table(slide_lengths)
    vmem = pl.BlockSpec(memory_space=pltpu.VMEM)

    def shape(count, width, kind=BF16):
        return jax.ShapeDtypeStruct((count, width), kind)

    packed = pl.pallas_call(
        functools.partial(pack_kernel, plan),
        in_specs=[vmem] * 3,
        out_specs=[vmem] * (2 * group),
        out_shape=[shape(rows, 3 * LANES)] * group + [shape(mid_rows, 2 * LANES)] * group,
        name="pack",
    )(queries, keys, values)
    mains, mids = packed[:group], packed[group:]
    mains = [mains[0]] + [exchange(mains[x], "inner", x) for x in range(1, group)]
    others = [exchange(mids[x & (group - 1)], "inner", x) for x in range(group, plan.inner)]
    top_own = jnp.concatenate(
        [main[: plan.top_rows, LANES:] for main in mains]
        + [other[: plan.top_rows] for other in others],
        axis=0,
    )
    tops = [exchange(top_own, "outer", x) for x in range(1, plan.outer)]

    count = group * rows
    local = pl.pallas_call(
        functools.partial(local_kernel, plan),
        in_specs=[vmem] * (1 + group),
        out_specs=[vmem] * (group + 3),
        out_shape=[shape(rows - mid_rows, LANES)] * group
        + [shape(group * mid_rows, LANES, F32)] * 3,
        scratch_shapes=[pltpu.VMEM((2, count, LANES), BF16)] * 5,
        name="local",
    )(table, *mains)
    rests, state = local[:group], local[group:]
    rests = [rests[0]] + [exchange(rests[x], "inner", x) for x in range(1, group)]

    first = pl.BlockSpec((mid_rows, LANES), lambda i: (0, 0))

    def whole(array):
        return pl.BlockSpec(array.shape, lambda i: (0, 0))

    operands = [table, *state]
    tail = [*others, *tops]
    upper = pl.pallas_call(
        functools.partial(upper_kernel, plan),
        grid=(1,),
        in_specs=[whole(a) for a in operands] + [first] * group + [whole(a) for a in tail],
        out_specs=[first] * group,
        out_shape=[shape(mid_rows, LANES)] * group,
        name="upper",
    )(*operands, *mains, *tail)
    upper = [upper[0]] + [exchange(upper[x], "inner", x) for x in range(1, group)]

    return pl.pallas_call(
        functools.partial(project_kernel, plan),
        in_specs=[vmem] * (1 + 2 * group),
        out_specs=vmem,
        out_shape=shape(rows, out_weight.shape[1]),
        scratch_shapes=[pltpu.VMEM((rows, HEADS * HEAD_DIM), BF16)],
        name="project",
    )(out_weight, *upper, *rests)


def solution(mesh):
    tokens = P(("outer", "inner"), None)
    return jax.shard_map(
        shards,
        mesh=mesh,
        in_specs=(tokens, tokens, tokens, P(), P()),
        out_specs=tokens,
        check_vma=False,
    )
```

```python
import functools

import jax
import jax.numpy as jnp
from jax import lax
from jax.experimental import pallas as pl
from jax.experimental.pallas import tpu as pltpu
from jax.sharding import PartitionSpec as P

HEADS = 8
HEAD_DIM = 64
SPARSE = 1024
LANES = 128
FAR = 1 << 30
BARRED = -(2.0**100)
F32 = jnp.float32
BF16 = jnp.bfloat16


def exchange(block, axis, distance):
    count = lax.axis_size(axis)
    return lax.ppermute(block, axis, [(i, i ^ distance) for i in range(count)])


def shift_of(value):
    return value.bit_length() - 1


class Plan:
    def __init__(self, rows, inner, outer):
        self.rows = rows
        self.inner = inner
        self.outer = outer
        self.mid = rows * inner // SPARSE
        self.top = self.mid * outer
        self.group = SPARSE // rows
        self.mid_rows = rows // self.mid
        self.top_rows = rows // self.top
        self.top_tile = max(16, self.top_rows)
        assert HEADS == 2 * self.group and 2 * HEAD_DIM == LANES

    def me(self):
        return lax.axis_index("outer") * self.inner + lax.axis_index("inner")

    def pair(self):
        return lax.axis_index("inner") & (self.group - 1)

    def source_row(self, k):
        a = k >> shift_of(self.mid_rows)
        c = (k & (self.mid_rows - 1)) >> shift_of(self.top_rows)
        b = k & (self.top_rows - 1)
        return self.top * b + self.mid * c + a


def dot(a, b, dims):
    return lax.dot_general(a, b, (dims, ((), ())), preferred_element_type=F32)


def pick(wrapped, head, rows):
    return jnp.where(wrapped == ((rows - head) & (rows - 1)), 1.0, 0.0).astype(BF16)


def pack_kernel(plan, slots, q_ref, k_ref, v_ref, *refs):
    rows, n = plan.rows, len(slots)
    outs, (taken, sems) = refs[: 3 * n], refs[3 * n :]
    copies = []
    for s, x in enumerate(slots):
        columns = pl.ds(pl.multiple_of((plan.pair() ^ x) * LANES, LANES), LANES)
        for part, ref in enumerate((q_ref, k_ref, v_ref)):
            copy = pltpu.make_async_copy(
                ref.at[:, columns], taken.at[s, part], sems.at[s, part]
            )
            copy.start()
            copies.append(copy)
    k = lax.broadcasted_iota(jnp.int32, (rows, rows), 0)
    i = lax.broadcasted_iota(jnp.int32, (rows, rows), 1)
    wrapped = (plan.source_row(k) - i) & (rows - 1)
    first = lax.broadcasted_iota(jnp.int32, (rows, LANES), 1) < HEAD_DIM
    for s, x in enumerate(slots):
        pair = plan.pair() ^ x
        one_hot = [pick(wrapped, 2 * pair + t, rows) for t in range(2)]
        for part in range(3):
            copies[3 * s + part].wait()
        block = jnp.concatenate([taken[s, part] for part in range(3)], axis=1)
        one, two = [dot(m, block, ((1,), (0,))) for m in one_hot]
        query = jnp.where(first, one[:, :LANES], two[:, :LANES]) * HEAD_DIM**-0.5
        kv_one = jnp.where(
            first, one[:, LANES : 2 * LANES], pltpu.roll(one[:, 2 * LANES :], HEAD_DIM, axis=1)
        ).astype(BF16)
        kv_two = jnp.where(
            first, pltpu.roll(two[:, 2 * LANES :], HEAD_DIM, axis=1), two[:, LANES : 2 * LANES]
        ).astype(BF16)
        lead, second, mid = outs[3 * s : 3 * s + 3]
        lead[:, :LANES] = query.astype(BF16)
        lead[:, LANES:] = kv_one
        second[...] = kv_two
        mid[:, :LANES] = kv_one[: plan.mid_rows]
        mid[:, LANES:] = kv_two[: plan.mid_rows]


def features(plan, table_ref, t, base, slot_shift, count):
    r = lax.broadcasted_iota(jnp.int32, (count, LANES), 0)
    lane = lax.broadcasted_iota(jnp.int32, (count, LANES), 1)
    head = 2 * plan.pair() + t
    source = plan.me() ^ (base + (r >> slot_shift))
    k = r & ((1 << slot_shift) - 1)
    position = source * plan.rows + ((plan.source_row(k) + head) & (plan.rows - 1))
    starts = table_ref[2 * t : 2 * t + 1, :]
    ends = table_ref[2 * t + 1 : 2 * t + 2, :]
    inside = (position >= starts) & (position < ends)
    own = (lane < HEAD_DIM) if t == 0 else (lane >= HEAD_DIM)
    return inside, own


def as_query(block, inside, own):
    return jnp.where(own, block.astype(F32), jnp.where(inside, BARRED, 0.0)).astype(BF16)


def as_key(block, inside, own):
    return jnp.where(own, block.astype(F32), jnp.where(inside, 0.0, 1.0)).astype(BF16)


def as_value(block, own):
    return jnp.where(own, 1.0, block.astype(F32))


def row_iota(count):
    return lax.broadcasted_iota(jnp.int32, (count, LANES), 0)


def share(sums):
    return pltpu.roll(sums, HEAD_DIM, axis=1) / sums


def local_kernel(plan, t, table_ref, *refs):
    rows, group, mid_rows, tile = plan.rows, plan.group, plan.mid_rows, plan.top_tile
    leads, refs = refs[:group], refs[group:]
    if t:
        seconds, before, refs = refs[:group], refs[group], refs[group + 1 :]
        rests, refs = refs[:group], refs[group:]
    else:
        rest, refs = refs[0], refs[1:]
    sums_ref, maxima_ref, q_s, k_s, v_s, v2_s, vt_s = refs
    row = row_iota(rows)
    for x in range(group):
        here = pl.ds(x * rows, rows)
        inside, own = features(plan, table_ref, t, x, shift_of(rows), rows)
        kv = seconds[x][...] if t else leads[x][:, LANES:]
        q_s[here, :] = as_query(leads[x][:, :LANES], inside, own)
        k_s[here, :] = as_key(kv, inside, own)
        value = as_value(kv, own)
        v_s[here, :] = value.astype(BF16)
        v2_s[here, :] = jnp.where(row < mid_rows, 2.0 * value, value).astype(BF16)
        vt_s[here, :] = jnp.where(row < plan.top_rows, value, 0.0).astype(BF16)
    lane = lax.broadcasted_iota(jnp.int32, (rows - mid_rows, LANES), 1)
    for x in range(group):
        here = pl.ds(x * rows, rows)
        mid_here = pl.ds(x * mid_rows, mid_rows)
        rest_here = pl.ds(x * (rows - mid_rows), rows - mid_rows)
        scores = dot(q_s[here, :], k_s[...], ((1,), (1,)))
        largest = jnp.max(scores, axis=1, keepdims=True)
        probs = jnp.exp(scores - largest).astype(BF16)
        mid_sum = dot(probs[:mid_rows], v2_s[...], ((1,), (0,)))
        top_sum = dot(probs[:tile], vt_s[...], ((1,), (0,)))
        rest_sum = share(dot(probs[mid_rows:], v_s[...], ((1,), (0,))))
        top_sum = jnp.where(row_iota(tile) < plan.top_rows, top_sum, 0.0)
        sums_ref[mid_here, :] = mid_sum
        sums_ref[pl.ds(x * mid_rows, tile), :] += top_sum
        maxima_ref[mid_here, :] = jnp.broadcast_to(largest[:mid_rows], (mid_rows, LANES))
        if t:
            both = jnp.where(lane < HEAD_DIM, before[rest_here, :], rest_sum)
            rests[x][...] = both.astype(BF16)
        else:
            rest[rest_here, :] = rest_sum


def mid_kernel(plan, table_ref, *refs):
    group, mid_rows, tile = plan.group, plan.mid_rows, plan.top_tile
    states, refs = refs[:4], refs[4:]
    leads, refs = refs[:group], refs[group:]
    rests, refs = refs[:group], refs[group:]
    mids, refs = refs[: plan.inner - group], refs[plan.inner - group :]
    outs, lead_states = refs[:group], refs[group:]
    count = group * mid_rows
    queries = jnp.concatenate([lead[:mid_rows, :LANES] for lead in leads], axis=0)
    results = []
    for t in range(2):
        inside, own = features(plan, table_ref, t, 0, shift_of(mid_rows), count)
        q = as_query(queries, inside, own)
        kv = jnp.concatenate([mid[:, t * LANES : (t + 1) * LANES] for mid in mids], axis=0)
        n = kv.shape[0]
        inside, own = features(plan, table_ref, t, group, shift_of(mid_rows), n)
        value = as_value(kv, own)
        is_top = (row_iota(n) & (mid_rows - 1)) < plan.top_rows
        top_value = jnp.where(is_top, value, 0.0).astype(BF16)
        old = states[2 * t + 1][:, :1]
        scores = dot(q, as_key(kv, inside, own), ((1,), (1,)))
        new = jnp.maximum(old, jnp.max(scores, axis=1, keepdims=True))
        probs = jnp.exp(scores - new).astype(BF16)
        sums = states[2 * t][...] * jnp.exp(old - new)
        sums = sums + dot(probs, value.astype(BF16), ((1,), (0,)))

        def leading(array):
            return jnp.concatenate(
                [array[x * mid_rows : x * mid_rows + tile] for x in range(group)], axis=0
            )

        extra = dot(leading(probs), top_value, ((1,), (0,)))
        lead_states[3 * t][...] = leading(sums) + extra
        lead_states[3 * t + 1][...] = jnp.broadcast_to(leading(new), (group * tile, LANES))
        lead_states[3 * t + 2][...] = leading(q)
        if plan.top_rows < tile:
            keep = (row_iota(group * tile) & (tile - 1)) < plan.top_rows
            lead_states[3 * t][...] = leading(sums) + jnp.where(keep, extra, 0.0)
        results.append(share(sums))
    lane = lax.broadcasted_iota(jnp.int32, (count, LANES), 1)
    both = jnp.where(lane < HEAD_DIM, results[0], results[1]).astype(BF16)
    for x in range(group):
        outs[x][: mid_rows - tile] = both[x * mid_rows + tile : (x + 1) * mid_rows]
        outs[x][mid_rows - tile :] = rests[x][...]


def top_kernel(plan, table_ref, *refs):
    group, tile = plan.group, plan.top_tile
    states, refs = refs[:6], refs[6:]
    tops, outs = refs[: plan.outer - 1], refs[plan.outer - 1 :]
    count = group * tile
    shift = shift_of(plan.top_rows)
    is_top = (row_iota(count) & (tile - 1)) < plan.top_rows
    results = []
    for t in range(2):
        keys, values = [], []
        for e in range(1, plan.outer):
            kv = tops[e - 1][:, t * LANES : (t + 1) * LANES]
            inside, own = features(plan, table_ref, t, e * plan.inner, shift, kv.shape[0])
            keys.append(as_key(kv, inside, own))
            values.append(as_value(kv, own).astype(BF16))
        sums, old, q = states[3 * t][...], states[3 * t + 1][:, :1], states[3 * t + 2][...]
        scores = dot(q, jnp.concatenate(keys, axis=0), ((1,), (1,)))
        new = jnp.maximum(old, jnp.max(scores, axis=1, keepdims=True))
        probs = jnp.exp(scores - new).astype(BF16)
        merged = sums * jnp.exp(old - new)
        merged = merged + dot(probs, jnp.concatenate(values, axis=0), ((1,), (0,)))
        results.append(share(jnp.where(is_top, merged, sums)))
    lane = lax.broadcasted_iota(jnp.int32, (count, LANES), 1)
    both = jnp.where(lane < HEAD_DIM, results[0], results[1]).astype(BF16)
    for x in range(group):
        outs[x][...] = both[x * tile : (x + 1) * tile]


def project_kernel(plan, weight_ref, *refs):
    rows, group = plan.rows, plan.group
    tops, mids, (out_ref, flat) = refs[:group], refs[group : 2 * group], refs[2 * group :]
    i = lax.broadcasted_iota(jnp.int32, (rows, rows), 0)
    k = lax.broadcasted_iota(jnp.int32, (rows, rows), 1)
    wrapped = (plan.source_row(k) - i) & (rows - 1)
    lane = lax.broadcasted_iota(jnp.int32, (rows, LANES), 1)
    for x in range(group):
        pair = plan.pair() ^ x
        block = jnp.concatenate([tops[x][...], mids[x][...]], axis=0)
        one = dot(pick(wrapped, 2 * pair, rows), block, ((1,), (0,)))
        two = dot(pick(wrapped, 2 * pair + 1, rows), block, ((1,), (0,)))
        columns = pl.ds(pl.multiple_of(pair * LANES, LANES), LANES)
        flat[:, columns] = jnp.where(lane < HEAD_DIM, one, two).astype(BF16)
    out_ref[...] = dot(flat[...], weight_ref[...], ((1,), (0,))).astype(BF16)


def slide_table(slide_lengths):
    slides = slide_lengths.shape[0]
    lane = jnp.arange(LANES, dtype=jnp.int32)
    index = jnp.arange(slides, dtype=jnp.int32)
    table = []
    for t in range(2):
        slide = lane - (HEAD_DIM if t == 0 else 0)
        valid = (slide >= 0) & (slide < slides)
        for bound in range(2):
            before = index[None, :] < (slide + bound)[:, None]
            total = jnp.sum(jnp.where(before, slide_lengths[None, :], 0), axis=1)
            table.append(jnp.where(valid, total, FAR))
    return jnp.stack(table + table, axis=0).astype(jnp.int32)


def shape(count, width, kind=BF16):
    return jax.ShapeDtypeStruct((count, width), kind)


def call(kernel, operands, results, scratch=(), in_specs=None):
    vmem = pl.BlockSpec(memory_space=pltpu.VMEM)
    return pl.pallas_call(
        kernel,
        in_specs=in_specs or [vmem] * len(operands),
        out_specs=[vmem] * len(results),
        out_shape=results,
        scratch_shapes=scratch,
        compiler_params=pltpu.CompilerParams(vmem_limit_bytes=24 << 20),
    )(*operands)


def shards(queries, keys, values, out_weight, slide_lengths):
    plan = Plan(queries.shape[0], lax.axis_size("inner"), lax.axis_size("outer"))
    rows, group, mid_rows, tile = plan.rows, plan.group, plan.mid_rows, plan.top_tile
    table = slide_table(slide_lengths)

    held = [pltpu.with_memory_space_constraint(a, pltpu.HBM) for a in (queries, keys, values)]
    leads, seconds, mids = [None] * group, [None] * group, [None] * group
    for slots in (list(range(group // 2, group)), list(range(group // 2))):
        packed = call(
            functools.partial(pack_kernel, plan, slots),
            held,
            [shape(rows, 2 * LANES), shape(rows, LANES), shape(mid_rows, 2 * LANES)] * len(slots),
            [pltpu.VMEM((len(slots), 3, rows, LANES), BF16), pltpu.SemaphoreType.DMA((len(slots), 3))],
            [pl.BlockSpec(memory_space=pltpu.HBM)] * 3,
        )
        for s, x in enumerate(slots):
            leads[x], seconds[x], mids[x] = packed[3 * s : 3 * s + 3]
    leads = [leads[0]] + [exchange(leads[x], "inner", x) for x in range(1, group)]
    seconds = [seconds[0]] + [exchange(seconds[x], "inner", x) for x in range(1, group)]
    others = [exchange(mids[x & (group - 1)], "inner", x) for x in range(group, plan.inner)]

    own = jnp.concatenate(
        [
            jnp.concatenate([leads[x][: plan.top_rows, LANES:], seconds[x][: plan.top_rows]], axis=1)
            for x in range(group)
        ]
        + [other[: plan.top_rows] for other in others],
        axis=0,
    )
    tops = [exchange(own, "outer", x) for x in range(1, plan.outer)]

    count = group * rows
    scratch = [pltpu.VMEM((count, LANES), BF16)] * 5
    state = [shape(group * mid_rows, LANES, F32)] * 2
    rest_one, sums_one, maxima_one = call(
        functools.partial(local_kernel, plan, 0),
        (table, *leads),
        [shape(group * (rows - mid_rows), LANES, F32), *state],
        scratch,
    )
    *rests, sums_two, maxima_two = call(
        functools.partial(local_kernel, plan, 1),
        (table, *leads, *seconds, rest_one),
        [shape(rows - mid_rows, LANES)] * group + state,
        scratch,
    )
    lead_state = [shape(group * tile, LANES, F32)] * 2 + [shape(group * tile, LANES)]
    middle = call(
        functools.partial(mid_kernel, plan),
        (table, sums_one, maxima_one, sums_two, maxima_two, *leads, *rests, *others),
        [shape(rows - tile, LANES)] * group + lead_state * 2,
    )
    middles, lead_state = middle[:group], middle[group:]
    uppers = call(
        functools.partial(top_kernel, plan),
        (table, *lead_state, *tops),
        [shape(tile, LANES)] * group,
    )
    back = []
    for parts in (uppers, middles):
        back += [parts[0]] + [exchange(parts[x], "inner", x) for x in range(1, group)]
    return call(
        functools.partial(project_kernel, plan),
        (out_weight, *back),
        [shape(rows, out_weight.shape[1])],
        [pltpu.VMEM((rows, HEADS * HEAD_DIM), BF16)],
    )[0]


def solution(mesh):
    tokens = P(("outer", "inner"), None)

    return jax.shard_map(
        shards,
        mesh=mesh,
        in_specs=(tokens, tokens, tokens, P(), P()),
        out_specs=tokens,
        check_vma=False,
    )
```

```python
import functools

import jax
import jax.numpy as jnp
from jax import lax
from jax.experimental import pallas as pl
from jax.experimental.pallas import tpu as pltpu
from jax.sharding import PartitionSpec as P

HEADS = 8
HEAD_DIM = 64
SPARSE = 1024
LANES = 128
FAR = 1 << 30
BARRED = -(2.0**100)
F32 = jnp.float32
BF16 = jnp.bfloat16


def exchange(block, axis, distance):
    count = lax.axis_size(axis)
    return lax.ppermute(block, axis, [(i, i ^ distance) for i in range(count)])


def shift_of(value):
    return value.bit_length() - 1


class Plan:
    def __init__(self, rows, inner, outer):
        self.rows = rows
        self.inner = inner
        self.outer = outer
        self.mid = rows * inner // SPARSE
        self.top = self.mid * outer
        self.group = SPARSE // rows
        self.mid_rows = rows // self.mid
        self.top_rows = rows // self.top
        self.top_tile = max(16, self.top_rows)
        assert self.group == 4 and HEADS == 2 * self.group and 2 * HEAD_DIM == LANES

    def me(self):
        return lax.axis_index("outer") * self.inner + lax.axis_index("inner")

    def pair(self):
        return lax.axis_index("inner") & (self.group - 1)

    def source_row(self, k):
        a = k >> shift_of(self.mid_rows)
        c = (k & (self.mid_rows - 1)) >> shift_of(self.top_rows)
        b = k & (self.top_rows - 1)
        return self.top * b + self.mid * c + a


def dot(a, b, dims):
    return lax.dot_general(a, b, (dims, ((), ())), preferred_element_type=F32)


def pick(wrapped, head, rows):
    return jnp.where(wrapped == ((rows - head) & (rows - 1)), 1.0, 0.0).astype(BF16)


def pack_kernel(plan, lengths_ref, q_ref, k_ref, v_ref, *refs):
    rows, mid_rows, tile = plan.rows, plan.mid_rows, plan.top_tile
    own, near, *outs, table, taken, lengths, sems, length_sem = refs
    leads, seconds, heads, tails = [outs[n : n + 2] for n in range(0, 8, 2)]
    copies = []
    for x in (2, 3, 0, 1):
        columns = pl.ds(pl.multiple_of((plan.pair() ^ x) * LANES, LANES), LANES)
        for part, ref in enumerate((q_ref, k_ref, v_ref)):
            copy = pltpu.make_async_copy(ref.at[:, columns], taken.at[x, part], sems.at[x, part])
            copy.start()
            copies.append(copy)
    length_copy = pltpu.make_async_copy(lengths_ref, lengths, length_sem)
    length_copy.start()
    k = lax.broadcasted_iota(jnp.int32, (rows, rows), 0)
    i = lax.broadcasted_iota(jnp.int32, (rows, rows), 1)
    wrapped = (plan.source_row(k) - i) & (rows - 1)
    first = lax.broadcasted_iota(jnp.int32, (rows, LANES), 1) < HEAD_DIM
    for s, x in enumerate((2, 3, 0, 1)):
        pair = plan.pair() ^ x
        one_hot = [pick(wrapped, 2 * pair + t, rows) for t in range(2)]
        for part in range(3):
            copies[3 * s + part].wait()
        block = jnp.concatenate([taken[x, part] for part in range(3)], axis=1)
        one, two = [dot(m, block, ((1,), (0,))) for m in one_hot]
        query = jnp.where(first, one[:, :LANES], two[:, :LANES]) * HEAD_DIM**-0.5
        kv_one = jnp.where(
            first, one[:, LANES : 2 * LANES], pltpu.roll(one[:, 2 * LANES :], HEAD_DIM, axis=1)
        ).astype(BF16)
        kv_two = jnp.where(
            first, pltpu.roll(two[:, 2 * LANES :], HEAD_DIM, axis=1), two[:, LANES : 2 * LANES]
        ).astype(BF16)
        lead = leads[x - 2] if x >= 2 else (own, near)[x]
        lead[:, :LANES] = query.astype(BF16)
        lead[:, LANES : 2 * LANES] = kv_one
        if x >= 2:
            seconds[x - 2][...] = kv_two
        else:
            lead[:, 2 * LANES :] = kv_two
        at = (x & 1) * 2 * LANES
        for out, low, high in ((heads[x >> 1], 0, tile), (tails[x >> 1], tile, mid_rows)):
            out[:, at : at + LANES] = kv_one[low:high]
            out[:, at + LANES : at + 2 * LANES] = kv_two[low:high]
    length_copy.wait()
    slide_table(lengths, table)


def block_positions(plan, t, rows):
    head = 2 * plan.pair() + t
    return (plan.source_row(row_iota(rows)) + head) & (plan.rows - 1)


def block_inside(plan, table_ref, t, positions, slot):
    base = (plan.me() ^ slot) * plan.rows
    starts = table_ref[2 * t : 2 * t + 1, :] - base
    ends = table_ref[2 * t + 1 : 2 * t + 2, :] - base
    return (positions >= starts) & (positions < ends)


def features(plan, table_ref, t, base, slot_shift, count):
    r = lax.broadcasted_iota(jnp.int32, (count, LANES), 0)
    lane = lax.broadcasted_iota(jnp.int32, (count, LANES), 1)
    head = 2 * plan.pair() + t
    source = plan.me() ^ (base + (r >> slot_shift))
    k = r & ((1 << slot_shift) - 1)
    position = source * plan.rows + ((plan.source_row(k) + head) & (plan.rows - 1))
    starts = table_ref[2 * t : 2 * t + 1, :]
    ends = table_ref[2 * t + 1 : 2 * t + 2, :]
    inside = (position >= starts) & (position < ends)
    own = (lane < HEAD_DIM) if t == 0 else (lane >= HEAD_DIM)
    return inside, own


def as_query(block, inside, own):
    return jnp.where(own, block.astype(F32), jnp.where(inside, BARRED, 0.0)).astype(BF16)


def as_key(block, inside, own):
    return jnp.where(own, block.astype(F32), jnp.where(inside, 0.0, 1.0)).astype(BF16)


def as_value(block, own):
    return jnp.where(own, 1.0, block.astype(F32))


def row_iota(count):
    return lax.broadcasted_iota(jnp.int32, (count, LANES), 0)


def share(sums):
    return pltpu.roll(sums, HEAD_DIM, axis=1) / sums


def chunks(own, near, leads, seconds):
    part = lambda ref, n: ref.at[:, n * LANES : (n + 1) * LANES]
    queries = [part(ref, 0) for ref in (own, near, *leads)]
    firsts = [part(ref, 1) for ref in (own, near, *leads)]
    return queries, firsts, [part(own, 2), part(near, 2), *seconds]


def local_kernel(plan, t, table_ref, own, near, *refs):
    rows, group, mid_rows, tile = plan.rows, plan.group, plan.mid_rows, plan.top_tile
    leads, seconds, refs = refs[:2], refs[2 : 2 + 2 * t], refs[2 + 2 * t :]
    if t:
        before, rests, refs = refs[0], refs[1 : 1 + group], refs[1 + group :]
    else:
        rest, refs = refs[0], refs[1:]
    sums_ref, maxima_ref, q_s, k_s, v_s, v2_s, vt_s = refs
    queries, firsts, seconds = chunks(own, near, leads, seconds)
    positions = block_positions(plan, t, rows)
    lane = lax.broadcasted_iota(jnp.int32, (rows, LANES), 1)
    keys = (lane < HEAD_DIM) if t == 0 else (lane >= HEAD_DIM)
    is_top = row_iota(mid_rows) < plan.top_rows
    for x in range(group):
        here = pl.ds(x * rows, rows)
        mid_here = pl.ds(x * mid_rows, mid_rows)
        inside = block_inside(plan, table_ref, t, positions, x)
        kv = (seconds if t else firsts)[x][...].astype(F32)
        q_s[here, :] = as_query(queries[x][...], inside, keys)
        k_s[here, :] = as_key(kv, inside, keys)
        value = as_value(kv, keys)
        low = value.astype(BF16)
        v_s[here, :] = low
        v2_s[pl.ds(x * rows, mid_rows), :] = (2.0 * value[:mid_rows]).astype(BF16)
        v2_s[pl.ds(x * rows + mid_rows, rows - mid_rows), :] = low[mid_rows:]
        vt_s[mid_here, :] = jnp.where(is_top, value[:mid_rows], 0.0).astype(BF16)
    lane = lax.broadcasted_iota(jnp.int32, (rows - mid_rows, LANES), 1)
    for x in range(group):
        here = pl.ds(x * rows, rows)
        mid_here = pl.ds(x * mid_rows, mid_rows)
        rest_here = pl.ds(x * (rows - mid_rows), rows - mid_rows)
        scores = dot(q_s[here, :], k_s[...], ((1,), (1,)))
        largest = jnp.max(scores, axis=1, keepdims=True)
        probs = jnp.exp(scores - largest).astype(BF16)
        mid_sum = dot(probs[:mid_rows], v2_s[...], ((1,), (0,)))
        top_probs = [probs[:tile, y * rows : y * rows + mid_rows] for y in range(group)]
        top_sum = dot(jnp.concatenate(top_probs, axis=1), vt_s[...], ((1,), (0,)))
        rest_sum = share(dot(probs[mid_rows:], v_s[...], ((1,), (0,))))
        top_sum = jnp.where(row_iota(tile) < plan.top_rows, top_sum, 0.0)
        sums_ref[mid_here, :] = mid_sum
        sums_ref[pl.ds(x * mid_rows, tile), :] += top_sum
        maxima_ref[mid_here, :] = jnp.broadcast_to(largest[:mid_rows], (mid_rows, LANES))
        if t:
            both = jnp.where(lane < HEAD_DIM, before[rest_here, :], rest_sum)
            rests[x][...] = both.astype(BF16)
        else:
            rest[rest_here, :] = rest_sum


def other_chunks(arrays):
    width = 2 * LANES
    slots = []
    for n in range(0, len(arrays), 2):
        if isinstance(arrays[n], jax.Array):
            slots += [arrays[n][:, :width], arrays[n + 1][:, width:]]
        else:
            slots += [arrays[n].at[:, :width], arrays[n + 1].at[:, width:]]
    return slots


def mid_kernel(plan, table_ref, *refs):
    group, mid_rows, tile = plan.group, plan.mid_rows, plan.top_tile
    n = plan.inner - group
    states, refs = refs[:4], refs[4:]
    queries, refs = [ref.at[:, :LANES] for ref in refs[:4]], refs[4:]
    heads, tails, refs = other_chunks(refs[:n]), other_chunks(refs[n : 2 * n]), refs[2 * n :]
    outs, lead_states, (k_s, v_s, vt_s) = refs[:group], refs[group : group + 6], refs[group + 6 :]
    count = group * mid_rows
    queries = jnp.concatenate([query[:mid_rows, :] for query in queries], axis=0)
    key_lane = lax.broadcasted_iota(jnp.int32, (mid_rows, LANES), 1)
    results = []
    for t in range(2):
        inside, own = features(plan, table_ref, t, 0, shift_of(mid_rows), count)
        q = as_query(queries, inside, own)
        positions = block_positions(plan, t, mid_rows)
        keys = (key_lane < HEAD_DIM) if t == 0 else (key_lane >= HEAD_DIM)
        columns = slice(t * LANES, (t + 1) * LANES)
        for y in range(n):
            inside = block_inside(plan, table_ref, t, positions, group + y)
            parts = (
                (heads[y], 0, tile, y * tile),
                (tails[y], tile, mid_rows, n * tile + y * (mid_rows - tile)),
            )
            for ref, low, high, at in parts:
                kv = ref[:, columns].astype(F32)
                there = pl.ds(at, high - low)
                value = as_value(kv, keys[low:high])
                k_s[there, :] = as_key(kv, inside[low:high], keys[low:high])
                v_s[there, :] = value.astype(BF16)
                if low == 0:
                    is_top = row_iota(tile) < plan.top_rows
                    vt_s[there, :] = jnp.where(is_top, value, 0.0).astype(BF16)
        old = states[2 * t + 1][:, :1]
        scores = dot(q, k_s[...], ((1,), (1,)))
        new = jnp.maximum(old, jnp.max(scores, axis=1, keepdims=True))
        probs = jnp.exp(scores - new).astype(BF16)
        sums = states[2 * t][...] * jnp.exp(old - new)
        sums = sums + dot(probs, v_s[...], ((1,), (0,)))

        def leading(array):
            return jnp.concatenate(
                [array[x * mid_rows : x * mid_rows + tile] for x in range(group)], axis=0
            )

        extra = dot(leading(probs[:, : n * tile]), vt_s[...], ((1,), (0,)))
        keep = (row_iota(group * tile) & (tile - 1)) < plan.top_rows
        lead_states[3 * t][...] = leading(sums) + jnp.where(keep, extra, 0.0)
        lead_states[3 * t + 1][...] = jnp.broadcast_to(leading(new), (group * tile, LANES))
        lead_states[3 * t + 2][...] = leading(q)
        results.append(share(sums))
    lane = lax.broadcasted_iota(jnp.int32, (count, LANES), 1)
    both = jnp.where(lane < HEAD_DIM, results[0], results[1]).astype(BF16)
    for x in range(group):
        outs[x][...] = both[x * mid_rows + tile : (x + 1) * mid_rows]


def top_kernel(plan, table_ref, *refs):
    group, tile = plan.group, plan.top_tile
    states, refs = refs[:6], refs[6:]
    middles, refs = refs[:group], refs[group:]
    tops, outs = refs[: plan.outer - 1], refs[plan.outer - 1 :]
    count = group * tile
    shift = shift_of(plan.top_rows)
    is_top = (row_iota(count) & (tile - 1)) < plan.top_rows
    results = []
    for t in range(2):
        keys, values = [], []
        for e in range(1, plan.outer):
            kv = tops[e - 1][:, t * LANES : (t + 1) * LANES]
            inside, own = features(plan, table_ref, t, e * plan.inner, shift, kv.shape[0])
            keys.append(as_key(kv, inside, own))
            values.append(as_value(kv, own).astype(BF16))
        sums, old, q = states[3 * t][...], states[3 * t + 1][:, :1], states[3 * t + 2][...]
        scores = dot(q, jnp.concatenate(keys, axis=0), ((1,), (1,)))
        new = jnp.maximum(old, jnp.max(scores, axis=1, keepdims=True))
        probs = jnp.exp(scores - new).astype(BF16)
        merged = sums * jnp.exp(old - new)
        merged = merged + dot(probs, jnp.concatenate(values, axis=0), ((1,), (0,)))
        results.append(share(jnp.where(is_top, merged, sums)))
    lane = lax.broadcasted_iota(jnp.int32, (count, LANES), 1)
    both = jnp.where(lane < HEAD_DIM, results[0], results[1]).astype(BF16)
    for x in range(group):
        outs[x][:tile] = both[x * tile : (x + 1) * tile]
        outs[x][tile:] = middles[x][...]


def unpermute(plan, parts, low, high, out):
    rows = plan.rows
    i = lax.broadcasted_iota(jnp.int32, (rows, high - low), 0)
    k = lax.broadcasted_iota(jnp.int32, (rows, high - low), 1) + low
    wrapped = (plan.source_row(k) - i) & (rows - 1)
    lane = lax.broadcasted_iota(jnp.int32, (rows, LANES), 1)
    for x in range(plan.group):
        pair = plan.pair() ^ x
        one = dot(pick(wrapped, 2 * pair, rows), parts[x][...], ((1,), (0,)))
        two = dot(pick(wrapped, 2 * pair + 1, rows), parts[x][...], ((1,), (0,)))
        columns = pl.ds(pl.multiple_of(pair * LANES, LANES), LANES)
        value = jnp.where(lane < HEAD_DIM, one, two)
        if low == 0:
            value = value + out[1][:, columns].astype(F32)
        out[0][:, columns] = value.astype(BF16)


def order_kernel(plan, *refs):
    unpermute(plan, refs[:-1], plan.mid_rows, plan.rows, (refs[-1],))


def project_kernel(plan, weight_ref, rest_ref, *refs):
    uppers, (out_ref, flat) = refs[: plan.group], refs[plan.group :]
    unpermute(plan, uppers, 0, plan.mid_rows, (flat, rest_ref))
    out_ref[...] = dot(flat[...], weight_ref[...], ((1,), (0,))).astype(BF16)


def slide_table(lengths_ref, table_ref):
    row = lax.broadcasted_iota(jnp.int32, (8, LANES), 0)
    lane = lax.broadcasted_iota(jnp.int32, (8, LANES), 1)
    slide = lane - jnp.where(row < 2, HEAD_DIM, 0)
    table = jnp.full((8, LANES), FAR, jnp.int32)
    start = jnp.int32(0)
    for s in range(lengths_ref.shape[0]):
        end = start + lengths_ref[s]
        table = jnp.where(slide == s, jnp.where((row & 1) == 1, end, start), table)
        start = end
    table_ref[...] = table


def shape(count, width, kind=BF16):
    return jax.ShapeDtypeStruct((count, width), kind)


def call(kernel, operands, results, scratch=(), in_specs=None):
    vmem = pl.BlockSpec(memory_space=pltpu.VMEM)
    return pl.pallas_call(
        kernel,
        in_specs=in_specs or [vmem] * len(operands),
        out_specs=[vmem] * len(results),
        out_shape=results,
        scratch_shapes=scratch,
        compiler_params=pltpu.CompilerParams(vmem_limit_bytes=24 << 20),
    )(*operands)


def shards(queries, keys, values, out_weight, slide_lengths):
    plan = Plan(queries.shape[0], lax.axis_size("inner"), lax.axis_size("outer"))
    rows, group, mid_rows, tile = plan.rows, plan.group, plan.mid_rows, plan.top_tile
    hbm = pl.BlockSpec(memory_space=pltpu.HBM)
    own, near, *packed, table = call(
        functools.partial(pack_kernel, plan),
        [
            pltpu.with_memory_space_constraint(a, pltpu.HBM)
            for a in (slide_lengths, queries, keys, values)
        ],
        [shape(rows, 3 * LANES)] * 2
        + [shape(rows, 2 * LANES)] * 2
        + [shape(rows, LANES)] * 2
        + [shape(tile, 4 * LANES)] * 2
        + [shape(mid_rows - tile, 4 * LANES)] * 2
        + [shape(8, LANES, jnp.int32)],
        [
            pltpu.VMEM((group, 3, rows, LANES), BF16),
            pltpu.SMEM(slide_lengths.shape, jnp.int32),
            pltpu.SemaphoreType.DMA((group, 3)),
            pltpu.SemaphoreType.DMA,
        ],
        [hbm] * 4,
    )
    leads, seconds, heads, tails = [packed[n : n + 2] for n in range(0, 8, 2)]
    leads = [exchange(leads[n], "inner", 2 + n) for n in range(2)]
    seconds = [exchange(seconds[n], "inner", 2 + n) for n in range(2)]
    near = exchange(near, "inner", 1)
    other_heads, other_tails = [], []
    for x in range(group, plan.inner, 2):
        for parts, slots in ((heads, other_heads), (tails, other_tails)):
            other = exchange(parts[x >> 1 & 1], "inner", x)
            slots += [other, exchange(other, "inner", 1)]

    top = plan.top_rows
    firsts = [a[:top, LANES : 2 * LANES] for a in (own, near, *leads)]
    lasts = [a[:top, 2 * LANES :] for a in (own, near)] + [a[:top] for a in seconds]
    kv = [jnp.concatenate(slot, axis=1) for slot in zip(firsts, lasts)]
    top_own = jnp.concatenate(kv + [slot[:top] for slot in other_chunks(other_heads)], axis=0)
    tops = [exchange(top_own, "outer", x) for x in range(1, plan.outer)]

    count = group * rows
    scratch = [pltpu.VMEM((count, LANES), BF16)] * 4
    scratch += [pltpu.VMEM((group * mid_rows, LANES), BF16)]
    state = [shape(group * mid_rows, LANES, F32)] * 2
    rest_one, sums_one, maxima_one = call(
        functools.partial(local_kernel, plan, 0),
        (table, own, near, *leads),
        [shape(group * (rows - mid_rows), LANES, F32), *state],
        scratch,
    )
    *rests, sums_two, maxima_two = call(
        functools.partial(local_kernel, plan, 1),
        (table, own, near, *leads, *seconds, rest_one),
        [shape(rows - mid_rows, LANES)] * group + state,
        scratch,
    )
    rests = [rests[0]] + [exchange(rests[x], "inner", x) for x in range(1, group)]
    lead_state = [shape(group * tile, LANES, F32)] * 2 + [shape(group * tile, LANES)]
    n_mid = (plan.inner - group) * mid_rows
    middle = call(
        functools.partial(mid_kernel, plan),
        (
            table,
            *(sums_one, maxima_one, sums_two, maxima_two),
            *(own, near, *leads),
            *other_heads,
            *other_tails,
        ),
        [shape(mid_rows - tile, LANES)] * group + lead_state * 2,
        [pltpu.VMEM((n_mid, LANES), BF16)] * 2
        + [pltpu.VMEM(((plan.inner - group) * tile, LANES), BF16)],
    )
    middles, lead_state = middle[:group], middle[group:]
    uppers = call(
        functools.partial(top_kernel, plan),
        (table, *lead_state, *middles, *tops),
        [shape(mid_rows, LANES)] * group,
    )
    uppers = [uppers[0]] + [exchange(uppers[x], "inner", x) for x in range(1, group)]
    ordered = call(functools.partial(order_kernel, plan), rests, [shape(rows, HEADS * HEAD_DIM)])[0]
    return call(
        functools.partial(project_kernel, plan),
        (out_weight, ordered, *uppers),
        [shape(rows, out_weight.shape[1])],
        [pltpu.VMEM((rows, HEADS * HEAD_DIM), BF16)],
    )[0]


def solution(mesh):
    tokens = P(("outer", "inner"), None)

    return jax.shard_map(
        shards,
        mesh=mesh,
        in_specs=(tokens, tokens, tokens, P(), P()),
        out_specs=tokens,
        check_vma=False,
    )
```

```python
import functools

import jax
import jax.numpy as jnp
from jax import lax
from jax.experimental import pallas as pl
from jax.experimental.pallas import tpu as pltpu
from jax.sharding import PartitionSpec as P

HEADS = 8
HEAD_DIM = 64
SPARSE = 1024
LANES = 128
FAR = 1 << 30
BARRED = -(2.0**100)
F32 = jnp.float32
BF16 = jnp.bfloat16


def exchange(block, axis, distance):
    count = lax.axis_size(axis)
    return lax.ppermute(block, axis, [(i, i ^ distance) for i in range(count)])


def shift_of(value):
    return value.bit_length() - 1


class Plan:
    def __init__(self, rows, inner, outer):
        self.rows = rows
        self.inner = inner
        self.outer = outer
        self.mid = rows * inner // SPARSE
        self.top = self.mid * outer
        self.group = SPARSE // rows
        self.mid_rows = rows // self.mid
        self.top_rows = rows // self.top
        self.top_tile = max(16, self.top_rows)
        assert self.group == 4 and HEADS == 2 * self.group and 2 * HEAD_DIM == LANES

    def me(self):
        return lax.axis_index("outer") * self.inner + lax.axis_index("inner")

    def pair(self):
        return lax.axis_index("inner") & (self.group - 1)

    def source_row(self, k):
        a = k >> shift_of(self.mid_rows)
        c = (k & (self.mid_rows - 1)) >> shift_of(self.top_rows)
        b = k & (self.top_rows - 1)
        return self.top * b + self.mid * c + a


def dot(a, b, dims):
    return lax.dot_general(a, b, (dims, ((), ())), preferred_element_type=F32)


def pick(wrapped, head, rows):
    return jnp.where(wrapped == ((rows - head) & (rows - 1)), 1.0, 0.0).astype(BF16)


def pack_kernel(plan, lengths_ref, q_ref, k_ref, v_ref, *refs):
    rows, mid_rows, tile = plan.rows, plan.mid_rows, plan.top_tile
    own, near, *outs, table, taken, lengths, sems, length_sem = refs
    leads, seconds, heads, tails = [outs[n : n + 2] for n in range(0, 8, 2)]
    copies = []
    for x in (2, 3, 0, 1):
        columns = pl.ds(pl.multiple_of((plan.pair() ^ x) * LANES, LANES), LANES)
        for part, ref in enumerate((q_ref, k_ref, v_ref)):
            copy = pltpu.make_async_copy(ref.at[:, columns], taken.at[x, part], sems.at[x, part])
            copy.start()
            copies.append(copy)
    length_copy = pltpu.make_async_copy(lengths_ref, lengths, length_sem)
    length_copy.start()
    k = lax.broadcasted_iota(jnp.int32, (rows, rows), 0)
    i = lax.broadcasted_iota(jnp.int32, (rows, rows), 1)
    wrapped = (plan.source_row(k) - i) & (rows - 1)
    first = lax.broadcasted_iota(jnp.int32, (rows, LANES), 1) < HEAD_DIM
    for s, x in enumerate((2, 3, 0, 1)):
        pair = plan.pair() ^ x
        one_hot = [pick(wrapped, 2 * pair + t, rows) for t in range(2)]
        if s % 2 == 0:
            for copy in copies[3 * s : 3 * s + 6]:
                copy.wait()
        block = jnp.concatenate([taken[x, part] for part in range(3)], axis=1)
        one, two = [dot(m, block, ((1,), (0,))) for m in one_hot]
        query = jnp.where(first, one[:, :LANES], two[:, :LANES]) * HEAD_DIM**-0.5
        kv_one = jnp.where(
            first, one[:, LANES : 2 * LANES], pltpu.roll(one[:, 2 * LANES :], HEAD_DIM, axis=1)
        ).astype(BF16)
        kv_two = jnp.where(
            first, pltpu.roll(two[:, 2 * LANES :], HEAD_DIM, axis=1), two[:, LANES : 2 * LANES]
        ).astype(BF16)
        lead = leads[x - 2] if x >= 2 else (own, near)[x]
        lead[:, :LANES] = query.astype(BF16)
        lead[:, LANES : 2 * LANES] = kv_one
        if x >= 2:
            seconds[x - 2][...] = kv_two
        else:
            lead[:, 2 * LANES :] = kv_two
        at = (x & 1) * 2 * LANES
        for out, low, high in ((heads[x >> 1], 0, tile), (tails[x >> 1], tile, mid_rows)):
            out[:, at : at + LANES] = kv_one[low:high]
            out[:, at + LANES : at + 2 * LANES] = kv_two[low:high]
    length_copy.wait()
    slide_table(lengths, table)


def block_positions(plan, t, rows):
    head = 2 * plan.pair() + t
    return (plan.source_row(row_iota(rows)) + head) & (plan.rows - 1)


def block_inside(plan, table_ref, t, positions, slot):
    base = (plan.me() ^ slot) * plan.rows
    starts = table_ref[2 * t : 2 * t + 1, :] - base
    ends = table_ref[2 * t + 1 : 2 * t + 2, :] - base
    return (positions >= starts) & (positions < ends)


def as_query(block, inside, own):
    return jnp.where(own, block.astype(F32), jnp.where(inside, BARRED, 0.0)).astype(BF16)


def as_key(block, inside, own):
    return jnp.where(own, block.astype(F32), jnp.where(inside, 0.0, 1.0)).astype(BF16)


def as_value(block, own):
    return jnp.where(own, 1.0, block.astype(F32))


def row_iota(count):
    return lax.broadcasted_iota(jnp.int32, (count, LANES), 0)


def share(sums):
    return pltpu.roll(sums, HEAD_DIM, axis=1) / sums


def chunks(own, near, leads, seconds):
    part = lambda ref, n: ref.at[:, n * LANES : (n + 1) * LANES]
    queries = [part(ref, 0) for ref in (own, near, *leads)]
    firsts = [part(ref, 1) for ref in (own, near, *leads)]
    return queries, firsts, [part(own, 2), part(near, 2), *seconds]


def local_kernel(plan, t, table_ref, own, near, *refs):
    rows, group, mid_rows, tile = plan.rows, plan.group, plan.mid_rows, plan.top_tile
    leads, seconds, refs = refs[:2], refs[2 : 2 + 2 * t], refs[2 + 2 * t :]
    if t:
        before, rests, refs = refs[0], refs[1 : 1 + group], refs[1 + group :]
    else:
        rest, refs = refs[0], refs[1:]
    sums_ref, maxima_ref, q_mid, q_s, k_s, v_s, vt_s, s_s = refs
    queries, firsts, seconds = chunks(own, near, leads, seconds)
    positions = block_positions(plan, t, rows)
    lane = lax.broadcasted_iota(jnp.int32, (rows, LANES), 1)
    keys = (lane < HEAD_DIM) if t == 0 else (lane >= HEAD_DIM)
    is_top = row_iota(mid_rows) < plan.top_rows
    for x in range(group):
        here = pl.ds(x * rows, rows)
        mid_here = pl.ds(x * mid_rows, mid_rows)
        inside = block_inside(plan, table_ref, t, positions, x)
        kv = (seconds if t else firsts)[x][...].astype(F32)
        query = as_query(queries[x][...], inside, keys)
        q_s[here, :] = query
        q_mid[mid_here, :] = query[:mid_rows]
        k_s[here, :] = as_key(kv, inside, keys)
        value = as_value(kv, keys)
        low = value.astype(BF16)
        v_s[here, :LANES] = low
        v_s[pl.ds(x * rows, mid_rows), LANES:] = (2.0 * value[:mid_rows]).astype(BF16)
        v_s[pl.ds(x * rows + mid_rows, rows - mid_rows), LANES:] = low[mid_rows:]
        vt_s[mid_here, :] = jnp.where(is_top, value[:mid_rows], 0.0).astype(BF16)
    lane = lax.broadcasted_iota(jnp.int32, (rows - mid_rows, LANES), 1)
    for x in range(group):
        here = pl.ds(x * rows, rows)
        mid_here = pl.ds(x * mid_rows, mid_rows)
        rest_here = pl.ds(x * (rows - mid_rows), rows - mid_rows)
        if x == 0:
            s_s[0] = dot(q_s[here, :], k_s[...], ((1,), (1,)))
        if x + 1 < group:
            there = pl.ds((x + 1) * rows, rows)
            s_s[(x + 1) % 2] = dot(q_s[there, :], k_s[...], ((1,), (1,)))
        scores = s_s[x % 2]
        largest = jnp.max(scores, axis=1, keepdims=True)
        probs = jnp.exp(scores - largest).astype(BF16)
        mid_sum = dot(probs[:mid_rows], v_s[:, LANES:], ((1,), (0,)))
        top_probs = [probs[:tile, y * rows : y * rows + mid_rows] for y in range(group)]
        top_sum = dot(jnp.concatenate(top_probs, axis=1), vt_s[...], ((1,), (0,)))
        rest_sum = share(dot(probs[mid_rows:], v_s[:, :LANES], ((1,), (0,))))
        top_sum = jnp.where(row_iota(tile) < plan.top_rows, top_sum, 0.0)
        sums_ref[mid_here, :] = mid_sum
        sums_ref[pl.ds(x * mid_rows, tile), :] += top_sum
        maxima_ref[mid_here, :] = jnp.broadcast_to(largest[:mid_rows], (mid_rows, LANES))
        if t:
            both = jnp.where(lane < HEAD_DIM, before[rest_here, :], rest_sum)
            rests[x][...] = both.astype(BF16)
        else:
            rest[rest_here, :] = rest_sum


def other_chunks(arrays):
    width = 2 * LANES
    slots = []
    for n in range(0, len(arrays), 2):
        if isinstance(arrays[n], jax.Array):
            slots += [arrays[n][:, :width], arrays[n + 1][:, width:]]
        else:
            slots += [arrays[n].at[:, :width], arrays[n + 1].at[:, width:]]
    return slots


def mid_kernel(plan, table_ref, *refs):
    group, mid_rows, tile = plan.group, plan.mid_rows, plan.top_tile
    n = plan.inner - group
    states, refs = refs[:6], refs[6:]
    heads, tails, refs = other_chunks(refs[:n]), other_chunks(refs[n : 2 * n]), refs[2 * n :]
    outs, lead_states, (k_s, v_s, vt_s, s_s) = refs[:group], refs[group : group + 6], refs[group + 6 :]
    count = group * mid_rows
    key_lane = lax.broadcasted_iota(jnp.int32, (mid_rows, LANES), 1)
    results = []
    for t in range(2):
        positions = block_positions(plan, t, mid_rows)
        keys = (key_lane < HEAD_DIM) if t == 0 else (key_lane >= HEAD_DIM)
        columns = slice(t * LANES, (t + 1) * LANES)
        for y in range(n):
            inside = block_inside(plan, table_ref, t, positions, group + y)
            parts = (
                (heads[y], 0, tile, y * tile),
                (tails[y], tile, mid_rows, n * tile + y * (mid_rows - tile)),
            )
            for ref, low, high, at in parts:
                kv = ref[:, columns].astype(F32)
                there = pl.ds(at, high - low)
                value = as_value(kv, keys[low:high])
                k_s[t, there, :] = as_key(kv, inside[low:high], keys[low:high])
                v_s[t, there, :] = value.astype(BF16)
                if low == 0:
                    is_top = row_iota(tile) < plan.top_rows
                    vt_s[t, there, :] = jnp.where(is_top, value, 0.0).astype(BF16)
        s_s[t] = dot(states[3 * t + 2][...], k_s[t], ((1,), (1,)))
    for t in range(2):
        old = states[3 * t + 1][...]
        scores = s_s[t]
        new = jnp.maximum(old, jnp.max(scores, axis=1, keepdims=True))
        probs = jnp.exp(scores - new[:, :1]).astype(BF16)
        sums = states[3 * t][...] * jnp.exp(old - new)
        sums = sums + dot(probs, v_s[t], ((1,), (0,)))

        def leading(array):
            return jnp.concatenate(
                [array[x * mid_rows : x * mid_rows + tile] for x in range(group)], axis=0
            )

        extra = dot(leading(probs[:, : n * tile]), vt_s[t], ((1,), (0,)))
        keep = (row_iota(group * tile) & (tile - 1)) < plan.top_rows
        lead_states[3 * t][...] = leading(sums) + jnp.where(keep, extra, 0.0)
        lead_states[3 * t + 1][...] = leading(new)
        lead_states[3 * t + 2][...] = leading(states[3 * t + 2])
        results.append(share(sums))
    lane = lax.broadcasted_iota(jnp.int32, (count, LANES), 1)
    both = jnp.where(lane < HEAD_DIM, results[0], results[1]).astype(BF16)
    for x in range(group):
        outs[x][...] = both[x * mid_rows + tile : (x + 1) * mid_rows]


def top_kernel(plan, table_ref, *refs):
    group, tile = plan.group, plan.top_tile
    states, refs = refs[:6], refs[6:]
    middles, refs = refs[:group], refs[group:]
    tops, refs = refs[: plan.outer - 1], refs[plan.outer - 1 :]
    outs, (k_s, v_s, s_s) = refs[:group], refs[group:]
    count = group * tile
    shift = shift_of(plan.top_rows)
    is_top = (row_iota(count) & (tile - 1)) < plan.top_rows
    n = tops[0].shape[0]
    row = row_iota(n)
    key_lane = lax.broadcasted_iota(jnp.int32, (n, LANES), 1)
    source = plan.me() ^ (row >> shift)
    bases = [(source ^ (e * plan.inner)) * plan.rows for e in range(1, plan.outer)]
    for t in range(2):
        keys = (key_lane < HEAD_DIM) if t == 0 else (key_lane >= HEAD_DIM)
        head = 2 * plan.pair() + t
        offset = (plan.source_row(row & (plan.top_rows - 1)) + head) & (plan.rows - 1)
        starts, ends = table_ref[2 * t : 2 * t + 1, :], table_ref[2 * t + 1 : 2 * t + 2, :]
        for e in range(1, plan.outer):
            kv = tops[e - 1][:, t * LANES : (t + 1) * LANES].astype(F32)
            position = bases[e - 1] + offset
            inside = (position >= starts) & (position < ends)
            there = pl.ds((e - 1) * n, n)
            k_s[t, there, :] = as_key(kv, inside, keys)
            v_s[t, there, :] = as_value(kv, keys).astype(BF16)
        s_s[t] = dot(states[3 * t + 2][...], k_s[t], ((1,), (1,)))
    results = []
    for t in range(2):
        sums, old = states[3 * t][...], states[3 * t + 1][...]
        scores = s_s[t]
        new = jnp.maximum(old, jnp.max(scores, axis=1, keepdims=True))
        probs = jnp.exp(scores - new[:, :1]).astype(BF16)
        merged = sums * jnp.exp(old - new) + dot(probs, v_s[t], ((1,), (0,)))
        results.append(share(jnp.where(is_top, merged, sums)))
    lane = lax.broadcasted_iota(jnp.int32, (count, LANES), 1)
    both = jnp.where(lane < HEAD_DIM, results[0], results[1]).astype(BF16)
    for x in range(group):
        outs[x][:tile] = both[x * tile : (x + 1) * tile]
        outs[x][tile:] = middles[x][...]


def unpermute(plan, parts, low, high, out):
    rows = plan.rows
    i = lax.broadcasted_iota(jnp.int32, (rows, high - low), 0)
    k = lax.broadcasted_iota(jnp.int32, (rows, high - low), 1) + low
    wrapped = (plan.source_row(k) - i) & (rows - 1)
    lane = lax.broadcasted_iota(jnp.int32, (rows, LANES), 1)
    for x in range(plan.group):
        pair = plan.pair() ^ x
        one = dot(pick(wrapped, 2 * pair, rows), parts[x][...], ((1,), (0,)))
        two = dot(pick(wrapped, 2 * pair + 1, rows), parts[x][...], ((1,), (0,)))
        columns = pl.ds(pl.multiple_of(pair * LANES, LANES), LANES)
        value = jnp.where(lane < HEAD_DIM, one, two)
        if low == 0:
            value = value + out[1][:, columns].astype(F32)
        out[0][:, columns] = value.astype(BF16)


def order_kernel(plan, *refs):
    unpermute(plan, refs[:-1], plan.mid_rows, plan.rows, (refs[-1],))


def project_kernel(plan, weight_ref, rest_ref, *refs):
    uppers, (out_ref, flat) = refs[: plan.group], refs[plan.group :]
    unpermute(plan, uppers, 0, plan.mid_rows, (flat, rest_ref))
    out_ref[...] = dot(flat[...], weight_ref[...], ((1,), (0,))).astype(BF16)


def slide_table(lengths_ref, table_ref):
    row = lax.broadcasted_iota(jnp.int32, (8, LANES), 0)
    lane = lax.broadcasted_iota(jnp.int32, (8, LANES), 1)
    slide = lane - jnp.where(row < 2, HEAD_DIM, 0)
    table = jnp.full((8, LANES), FAR, jnp.int32)
    start = jnp.int32(0)
    for s in range(lengths_ref.shape[0]):
        end = start + lengths_ref[s]
        table = jnp.where(slide == s, jnp.where((row & 1) == 1, end, start), table)
        start = end
    table_ref[...] = table


def shape(count, width, kind=BF16):
    return jax.ShapeDtypeStruct((count, width), kind)


def call(kernel, operands, results, scratch=(), in_specs=None):
    vmem = pl.BlockSpec(memory_space=pltpu.VMEM)
    return pl.pallas_call(
        kernel,
        in_specs=in_specs or [vmem] * len(operands),
        out_specs=[vmem] * len(results),
        out_shape=results,
        scratch_shapes=scratch,
        compiler_params=pltpu.CompilerParams(vmem_limit_bytes=24 << 20),
    )(*operands)


def shards(queries, keys, values, out_weight, slide_lengths):
    plan = Plan(queries.shape[0], lax.axis_size("inner"), lax.axis_size("outer"))
    rows, group, mid_rows, tile = plan.rows, plan.group, plan.mid_rows, plan.top_tile
    hbm = pl.BlockSpec(memory_space=pltpu.HBM)
    own, near, *packed, table = call(
        functools.partial(pack_kernel, plan),
        [
            pltpu.with_memory_space_constraint(a, pltpu.HBM)
            for a in (slide_lengths, queries, keys, values)
        ],
        [shape(rows, 3 * LANES)] * 2
        + [shape(rows, 2 * LANES)] * 2
        + [shape(rows, LANES)] * 2
        + [shape(tile, 4 * LANES)] * 2
        + [shape(mid_rows - tile, 4 * LANES)] * 2
        + [shape(8, LANES, jnp.int32)],
        [
            pltpu.VMEM((group, 3, rows, LANES), BF16),
            pltpu.SMEM(slide_lengths.shape, jnp.int32),
            pltpu.SemaphoreType.DMA((group, 3)),
            pltpu.SemaphoreType.DMA,
        ],
        [hbm] * 4,
    )
    leads, seconds, heads, tails = [packed[n : n + 2] for n in range(0, 8, 2)]
    leads = [exchange(leads[n], "inner", 2 + n) for n in range(2)]
    seconds = [exchange(seconds[n], "inner", 2 + n) for n in range(2)]
    near = exchange(near, "inner", 1)
    other_heads, other_tails = [], []
    for x in range(group, plan.inner, 2):
        for parts, slots in ((heads, other_heads), (tails, other_tails)):
            other = exchange(parts[x >> 1 & 1], "inner", x)
            slots += [other, exchange(other, "inner", 1)]

    top = plan.top_rows
    firsts = [a[:top, LANES : 2 * LANES] for a in (own, near, *leads)]
    lasts = [a[:top, 2 * LANES :] for a in (own, near)] + [a[:top] for a in seconds]
    kv = [jnp.concatenate(slot, axis=1) for slot in zip(firsts, lasts)]
    top_own = jnp.concatenate(kv + [slot[:top] for slot in other_chunks(other_heads)], axis=0)
    tops = [exchange(top_own, "outer", x) for x in range(1, plan.outer)]

    count = group * rows
    scratch = [pltpu.VMEM((count, LANES), BF16)] * 2
    scratch += [pltpu.VMEM((count, 2 * LANES), BF16)]
    scratch += [pltpu.VMEM((group * mid_rows, LANES), BF16)]
    scratch += [pltpu.VMEM((2, rows, count), F32)]
    state = [shape(group * mid_rows, LANES, F32)] * 2 + [shape(group * mid_rows, LANES)]
    rest_one, *state_one = call(
        functools.partial(local_kernel, plan, 0),
        (table, own, near, *leads),
        [shape(group * (rows - mid_rows), LANES, F32), *state],
        scratch,
    )
    local_two = call(
        functools.partial(local_kernel, plan, 1),
        (table, own, near, *leads, *seconds, rest_one),
        [shape(rows - mid_rows, LANES)] * group + state,
        scratch,
    )
    rests, state_two = local_two[:group], local_two[group:]
    rests = [rests[0]] + [exchange(rests[x], "inner", x) for x in range(1, group)]
    lead_state = [shape(group * tile, LANES, F32)] * 2 + [shape(group * tile, LANES)]
    n_top = (plan.outer - 1) * plan.inner * plan.top_rows
    n_mid = (plan.inner - group) * mid_rows
    middle = call(
        functools.partial(mid_kernel, plan),
        (
            table,
            *state_one,
            *state_two,
            *other_heads,
            *other_tails,
        ),
        [shape(mid_rows - tile, LANES)] * group + lead_state * 2,
        [pltpu.VMEM((2, n_mid, LANES), BF16)] * 2
        + [pltpu.VMEM((2, (plan.inner - group) * tile, LANES), BF16)]
        + [pltpu.VMEM((2, group * mid_rows, n_mid), F32)],
    )
    middles, lead_state = middle[:group], middle[group:]
    uppers = call(
        functools.partial(top_kernel, plan),
        (table, *lead_state, *middles, *tops),
        [shape(mid_rows, LANES)] * group,
        [pltpu.VMEM((2, n_top, LANES), BF16)] * 2
        + [pltpu.VMEM((2, group * tile, n_top), F32)],
    )
    uppers = [uppers[0]] + [exchange(uppers[x], "inner", x) for x in range(1, group)]
    ordered = call(functools.partial(order_kernel, plan), rests, [shape(rows, HEADS * HEAD_DIM)])[0]
    return call(
        functools.partial(project_kernel, plan),
        (out_weight, ordered, *uppers),
        [shape(rows, out_weight.shape[1])],
        [pltpu.VMEM((rows, HEADS * HEAD_DIM), BF16)],
    )[0]


def solution(mesh):
    tokens = P(("outer", "inner"), None)

    return jax.shard_map(
        shards,
        mesh=mesh,
        in_specs=(tokens, tokens, tokens, P(), P()),
        out_specs=tokens,
        check_vma=False,
    )
```

```python
import functools

import jax
import jax.numpy as jnp
from jax import lax
from jax.experimental import pallas as pl
from jax.experimental.pallas import tpu as pltpu
from jax.sharding import PartitionSpec as P

HEADS = 8
HEAD_DIM = 64
SPARSE = 1024
LANES = 128
FAR = 1 << 30
BARRED = -(2.0**100)
F32 = jnp.float32
BF16 = jnp.bfloat16


def exchange(block, axis, distance):
    count = lax.axis_size(axis)
    return lax.ppermute(block, axis, [(i, i ^ distance) for i in range(count)])


def shift_of(value):
    return value.bit_length() - 1


class Plan:
    def __init__(self, rows, inner, outer):
        self.rows = rows
        self.inner = inner
        self.outer = outer
        self.mid = rows * inner // SPARSE
        self.top = self.mid * outer
        self.group = SPARSE // rows
        self.mid_rows = rows // self.mid
        self.top_rows = rows // self.top
        self.top_tile = max(16, self.top_rows)
        assert self.group == 4 and HEADS == 2 * self.group and 2 * HEAD_DIM == LANES

    def me(self):
        return lax.axis_index("outer") * self.inner + lax.axis_index("inner")

    def pair(self):
        return lax.axis_index("inner") & (self.group - 1)

    def source_row(self, k):
        a = k >> shift_of(self.mid_rows)
        c = (k & (self.mid_rows - 1)) >> shift_of(self.top_rows)
        b = k & (self.top_rows - 1)
        return self.top * b + self.mid * c + a


def dot(a, b, dims):
    return lax.dot_general(a, b, (dims, ((), ())), preferred_element_type=F32)


def pick(wrapped, head, rows):
    return jnp.where(wrapped == ((rows - head) & (rows - 1)), 1.0, 0.0).astype(BF16)


def pack_kernel(plan, lengths_ref, q_ref, k_ref, v_ref, *refs):
    rows, mid_rows, tile = plan.rows, plan.mid_rows, plan.top_tile
    own, near, *outs, table, taken, one_hot, lengths, sems, length_sem = refs
    leads, seconds, heads, tails = [outs[n : n + 2] for n in range(0, 8, 2)]
    copies = []
    for x in (2, 3, 0, 1):
        columns = pl.ds(pl.multiple_of((plan.pair() ^ x) * LANES, LANES), LANES)
        for part, ref in enumerate((q_ref, k_ref, v_ref)):
            copy = pltpu.make_async_copy(ref.at[:, columns], taken.at[x, part], sems.at[x, part])
            copy.start()
            copies.append(copy)
    length_copy = pltpu.make_async_copy(lengths_ref, lengths, length_sem)
    length_copy.start()
    k = lax.broadcasted_iota(jnp.int32, (rows, rows), 0)
    i = lax.broadcasted_iota(jnp.int32, (rows, rows), 1)
    wrapped = (plan.source_row(k) - i) & (rows - 1)
    first = lax.broadcasted_iota(jnp.int32, (rows, LANES), 1) < HEAD_DIM
    for s, x in enumerate((2, 3, 0, 1)):
        for t in range(2):
            one_hot[s, t] = pick(wrapped, 2 * (plan.pair() ^ x) + t, rows)
    for s, x in enumerate((2, 3, 0, 1)):
        if s % 2 == 0:
            for copy in copies[3 * s : 3 * s + 6]:
                copy.wait()
        block = jnp.concatenate([taken[x, part] for part in range(3)], axis=1)
        one, two = [dot(one_hot[s, t], block, ((1,), (0,))) for t in range(2)]
        query = jnp.where(first, one[:, :LANES], two[:, :LANES]) * HEAD_DIM**-0.5
        kv_one = jnp.where(
            first, one[:, LANES : 2 * LANES], pltpu.roll(one[:, 2 * LANES :], HEAD_DIM, axis=1)
        ).astype(BF16)
        kv_two = jnp.where(
            first, pltpu.roll(two[:, 2 * LANES :], HEAD_DIM, axis=1), two[:, LANES : 2 * LANES]
        ).astype(BF16)
        if x >= 2:
            low, high = query[: rows // 2], pltpu.roll(query[rows // 2 :], HEAD_DIM, axis=1)
            leads[x - 2][:rows, :] = kv_one
            leads[x - 2][rows + tile :, :] = jnp.where(first[: rows // 2], low, high).astype(BF16)
            leads[x - 2][rows : rows + tile, :] = kv_two[:tile]
            seconds[x - 2][:rows, :] = kv_two
            seconds[x - 2][rows:, :] = jnp.where(first[: rows // 2], high, low).astype(BF16)
        else:
            out = (own, near)[x]
            out[:, :LANES] = query.astype(BF16)
            out[:, LANES : 2 * LANES] = kv_one
            out[:, 2 * LANES :] = kv_two
        at = (x & 1) * 2 * LANES
        for out, low, high in ((heads[x >> 1], 0, tile), (tails[x >> 1], tile, mid_rows)):
            out[:, at : at + LANES] = kv_one[low:high]
            out[:, at + LANES : at + 2 * LANES] = kv_two[low:high]
    length_copy.wait()
    slide_table(lengths, table)


def block_positions(plan, t, rows):
    head = 2 * plan.pair() + t
    return (plan.source_row(row_iota(rows)) + head) & (plan.rows - 1)


def block_inside(plan, table_ref, t, positions, slot):
    base = (plan.me() ^ slot) * plan.rows
    starts = table_ref[2 * t : 2 * t + 1, :] - base
    ends = table_ref[2 * t + 1 : 2 * t + 2, :] - base
    return (positions >= starts) & (positions < ends)


def as_query(block, inside, own):
    return jnp.where(own, block.astype(F32), jnp.where(inside, BARRED, 0.0)).astype(BF16)


def as_key(block, inside, own):
    return jnp.where(own, block.astype(F32), jnp.where(inside, 0.0, 1.0)).astype(BF16)


def as_value(block, own):
    return jnp.where(own, 1.0, block.astype(F32))


def row_iota(count):
    return lax.broadcasted_iota(jnp.int32, (count, LANES), 0)


def share(sums):
    return pltpu.roll(sums, HEAD_DIM, axis=1) / sums


def chunk(refs, x, t, rows):
    ref = refs[x]
    if x < 2:
        return ref[:, :LANES].astype(F32), ref[:, (1 + t) * LANES : (2 + t) * LANES]
    low = ref[ref.shape[0] - rows // 2 :, :].astype(F32)
    return jnp.concatenate([low, pltpu.roll(low, HEAD_DIM, axis=1)], axis=0), ref[:rows, :]


def local_kernel(plan, t, table_ref, *refs):
    rows, group, mid_rows, tile = plan.rows, plan.group, plan.mid_rows, plan.top_tile
    slots, refs = refs[:group], refs[group:]
    if t:
        before, rests, refs = refs[0], refs[1 : 1 + group], refs[1 + group :]
    else:
        rest, refs = refs[0], refs[1:]
    sums_ref, maxima_ref, q_mid, q_s, k_s, v_s, vt_s, s_s = refs
    positions = block_positions(plan, t, rows)
    lane = lax.broadcasted_iota(jnp.int32, (rows, LANES), 1)
    keys = (lane < HEAD_DIM) if t == 0 else (lane >= HEAD_DIM)
    is_top = row_iota(mid_rows) < plan.top_rows
    for x in range(group):
        here = pl.ds(x * rows, rows)
        mid_here = pl.ds(x * mid_rows, mid_rows)
        inside = block_inside(plan, table_ref, t, positions, x)
        query, kv = chunk(slots, x, t, rows)
        kv = kv.astype(F32)
        query = as_query(query, inside, keys)
        q_s[mid_here, :] = query[:mid_rows]
        q_mid[mid_here, :] = query[:mid_rows]
        others = rows - mid_rows
        q_s[pl.ds(group * mid_rows + x * others, others), :] = query[mid_rows:]
        k_s[here, :] = as_key(kv, inside, keys)
        value = as_value(kv, keys)
        low = value.astype(BF16)
        v_s[here, :LANES] = low
        v_s[pl.ds(x * rows, mid_rows), LANES:] = (2.0 * value[:mid_rows]).astype(BF16)
        v_s[pl.ds(x * rows + mid_rows, rows - mid_rows), LANES:] = low[mid_rows:]
        vt_s[mid_here, :] = jnp.where(is_top, value[:mid_rows], 0.0).astype(BF16)
    blocks = [(0, y) for y in range(0, group, 2)] + [(1, y) for y in range(0, group, 2)]
    sizes, first_row = (mid_rows, others), (0, group * mid_rows)

    def score(block):
        kind, y = block
        taken = q_s[pl.ds(first_row[kind] + y * sizes[kind], 2 * sizes[kind]), :]
        return dot(taken, k_s[...], ((1,), (1,)))

    def held(n):
        return s_s.at[n % 2, pl.ds(0, 2 * sizes[blocks[n][0]]), :]

    held(0)[...] = score(blocks[0])
    for n, (kind, y) in enumerate(blocks):
        if n + 1 < len(blocks):
            held(n + 1)[...] = score(blocks[n + 1])
        scores = held(n)[...]
        largest = jnp.max(scores, axis=1, keepdims=True)
        probs = jnp.exp(scores - largest).astype(BF16)
        there = pl.ds(y * sizes[kind], 2 * sizes[kind])
        if kind == 0:
            leads_of = [probs[z * mid_rows : z * mid_rows + tile] for z in range(2)]
            top_probs = jnp.concatenate(leads_of, axis=0)
            top_probs = jnp.concatenate(
                [top_probs[:, z * rows : z * rows + mid_rows] for z in range(group)], axis=1
            )
            sums_ref[there, :] = dot(probs, v_s[:, LANES:], ((1,), (0,)))
            top_sum = dot(top_probs, vt_s[...], ((1,), (0,)))
            for z in range(2):
                sums_ref[pl.ds((y + z) * mid_rows, tile), :] += jnp.where(
                    row_iota(tile) < plan.top_rows, top_sum[z * tile : (z + 1) * tile], 0.0
                )
            maxima_ref[there, :] = jnp.broadcast_to(largest, (2 * mid_rows, LANES))
        else:
            rest_sum = share(dot(probs, v_s[:, :LANES], ((1,), (0,))))
            if t:
                lane = lax.broadcasted_iota(jnp.int32, (2 * others, LANES), 1)
                both = jnp.where(lane < HEAD_DIM, before[there, :], rest_sum).astype(BF16)
                for z in range(2):
                    rests[y + z][...] = both[z * others : (z + 1) * others]
            else:
                rest[there, :] = rest_sum


def other_chunks(arrays):
    width = 2 * LANES
    slots = []
    for n in range(0, len(arrays), 2):
        if isinstance(arrays[n], jax.Array):
            slots += [arrays[n][:, :width], arrays[n + 1][:, width:]]
        else:
            slots += [arrays[n].at[:, :width], arrays[n + 1].at[:, width:]]
    return slots


def mid_kernel(plan, table_ref, *refs):
    group, mid_rows, tile = plan.group, plan.mid_rows, plan.top_tile
    n = plan.inner - group
    states, refs = refs[:6], refs[6:]
    heads, tails, refs = other_chunks(refs[:n]), other_chunks(refs[n : 2 * n]), refs[2 * n :]
    outs, lead_states, (k_s, v_s, vt_s, s_s) = refs[:group], refs[group : group + 6], refs[group + 6 :]
    count = group * mid_rows
    key_lane = lax.broadcasted_iota(jnp.int32, (mid_rows, LANES), 1)
    results = []
    for t in range(2):
        positions = block_positions(plan, t, mid_rows)
        keys = (key_lane < HEAD_DIM) if t == 0 else (key_lane >= HEAD_DIM)
        columns = slice(t * LANES, (t + 1) * LANES)
        for y in range(n):
            inside = block_inside(plan, table_ref, t, positions, group + y)
            parts = (
                (heads[y], 0, tile, y * tile),
                (tails[y], tile, mid_rows, n * tile + y * (mid_rows - tile)),
            )
            for ref, low, high, at in parts:
                kv = ref[:, columns].astype(F32)
                there = pl.ds(at, high - low)
                value = as_value(kv, keys[low:high])
                k_s[t, there, :] = as_key(kv, inside[low:high], keys[low:high])
                v_s[t, there, :] = value.astype(BF16)
                if low == 0:
                    is_top = row_iota(tile) < plan.top_rows
                    vt_s[t, there, :] = jnp.where(is_top, value, 0.0).astype(BF16)
        s_s[t] = dot(states[3 * t + 2][...], k_s[t], ((1,), (1,)))
    for t in range(2):
        old = states[3 * t + 1][...]
        scores = s_s[t]
        new = jnp.maximum(old, jnp.max(scores, axis=1, keepdims=True))
        probs = jnp.exp(scores - new[:, :1]).astype(BF16)
        sums = states[3 * t][...] * jnp.exp(old - new)
        sums = sums + dot(probs, v_s[t], ((1,), (0,)))

        def leading(array):
            return jnp.concatenate(
                [array[x * mid_rows : x * mid_rows + tile] for x in range(group)], axis=0
            )

        extra = dot(leading(probs[:, : n * tile]), vt_s[t], ((1,), (0,)))
        keep = (row_iota(group * tile) & (tile - 1)) < plan.top_rows
        lead_states[3 * t][...] = leading(sums) + jnp.where(keep, extra, 0.0)
        lead_states[3 * t + 1][...] = leading(new)
        lead_states[3 * t + 2][...] = leading(states[3 * t + 2])
        results.append(share(sums))
    lane = lax.broadcasted_iota(jnp.int32, (count, LANES), 1)
    both = jnp.where(lane < HEAD_DIM, results[0], results[1]).astype(BF16)
    for x in range(group):
        outs[x][...] = both[x * mid_rows + tile : (x + 1) * mid_rows]


def top_kernel(plan, table_ref, *refs):
    group, tile = plan.group, plan.top_tile
    states, refs = refs[:6], refs[6:]
    middles, refs = refs[:group], refs[group:]
    tops, refs = refs[: plan.outer - 1], refs[plan.outer - 1 :]
    outs, (k_s, v_s, s_s) = refs[:group], refs[group:]
    count = group * tile
    shift = shift_of(plan.top_rows)
    is_top = (row_iota(count) & (tile - 1)) < plan.top_rows
    n = tops[0].shape[0]
    row = row_iota(n)
    key_lane = lax.broadcasted_iota(jnp.int32, (n, LANES), 1)
    source = plan.me() ^ (row >> shift)
    bases = [(source ^ (e * plan.inner)) * plan.rows for e in range(1, plan.outer)]
    for t in range(2):
        keys = (key_lane < HEAD_DIM) if t == 0 else (key_lane >= HEAD_DIM)
        head = 2 * plan.pair() + t
        offset = (plan.source_row(row & (plan.top_rows - 1)) + head) & (plan.rows - 1)
        starts, ends = table_ref[2 * t : 2 * t + 1, :], table_ref[2 * t + 1 : 2 * t + 2, :]
        for e in range(1, plan.outer):
            kv = tops[e - 1][:, t * LANES : (t + 1) * LANES].astype(F32)
            position = bases[e - 1] + offset
            inside = (position >= starts) & (position < ends)
            there = pl.ds((e - 1) * n, n)
            k_s[t, there, :] = as_key(kv, inside, keys)
            v_s[t, there, :] = as_value(kv, keys).astype(BF16)
        s_s[t] = dot(states[3 * t + 2][...], k_s[t], ((1,), (1,)))
    results = []
    for t in range(2):
        sums, old = states[3 * t][...], states[3 * t + 1][...]
        scores = s_s[t]
        new = jnp.maximum(old, jnp.max(scores, axis=1, keepdims=True))
        probs = jnp.exp(scores - new[:, :1]).astype(BF16)
        merged = sums * jnp.exp(old - new) + dot(probs, v_s[t], ((1,), (0,)))
        results.append(share(jnp.where(is_top, merged, sums)))
    lane = lax.broadcasted_iota(jnp.int32, (count, LANES), 1)
    both = jnp.where(lane < HEAD_DIM, results[0], results[1]).astype(BF16)
    for x in range(group):
        outs[x][:tile] = both[x * tile : (x + 1) * tile]
        outs[x][tile:] = middles[x][...]


def unpermute(plan, parts, low, high, out):
    rows = plan.rows
    i = lax.broadcasted_iota(jnp.int32, (rows, high - low), 0)
    k = lax.broadcasted_iota(jnp.int32, (rows, high - low), 1) + low
    wrapped = (plan.source_row(k) - i) & (rows - 1)
    lane = lax.broadcasted_iota(jnp.int32, (rows, LANES), 1)
    for x in range(plan.group):
        pair = plan.pair() ^ x
        one = dot(pick(wrapped, 2 * pair, rows), parts[x][...], ((1,), (0,)))
        two = dot(pick(wrapped, 2 * pair + 1, rows), parts[x][...], ((1,), (0,)))
        columns = pl.ds(pl.multiple_of(pair * LANES, LANES), LANES)
        value = jnp.where(lane < HEAD_DIM, one, two)
        if low == 0:
            value = value + out[1][:, columns].astype(F32)
        out[0][:, columns] = value.astype(BF16)


def order_kernel(plan, *refs):
    unpermute(plan, refs[:-1], plan.mid_rows, plan.rows, (refs[-1],))


def project_kernel(plan, weight_ref, rest_ref, *refs):
    uppers, (out_ref, flat) = refs[: plan.group], refs[plan.group :]
    unpermute(plan, uppers, 0, plan.mid_rows, (flat, rest_ref))
    out_ref[...] = dot(flat[...], weight_ref[...], ((1,), (0,))).astype(BF16)


def slide_table(lengths_ref, table_ref):
    row = lax.broadcasted_iota(jnp.int32, (8, LANES), 0)
    lane = lax.broadcasted_iota(jnp.int32, (8, LANES), 1)
    slide = lane - jnp.where(row < 2, HEAD_DIM, 0)
    table = jnp.full((8, LANES), FAR, jnp.int32)
    start = jnp.int32(0)
    for s in range(lengths_ref.shape[0]):
        end = start + lengths_ref[s]
        table = jnp.where(slide == s, jnp.where((row & 1) == 1, end, start), table)
        start = end
    table_ref[...] = table


def shape(count, width, kind=BF16):
    return jax.ShapeDtypeStruct((count, width), kind)


def call(kernel, operands, results, scratch=(), in_specs=None):
    vmem = pl.BlockSpec(memory_space=pltpu.VMEM)
    return pl.pallas_call(
        kernel,
        in_specs=in_specs or [vmem] * len(operands),
        out_specs=[vmem] * len(results),
        out_shape=results,
        scratch_shapes=scratch,
        compiler_params=pltpu.CompilerParams(vmem_limit_bytes=24 << 20),
    )(*operands)


def shards(queries, keys, values, out_weight, slide_lengths):
    plan = Plan(queries.shape[0], lax.axis_size("inner"), lax.axis_size("outer"))
    rows, group, mid_rows, tile = plan.rows, plan.group, plan.mid_rows, plan.top_tile
    hbm = pl.BlockSpec(memory_space=pltpu.HBM)
    own, near, *packed, table = call(
        functools.partial(pack_kernel, plan),
        [
            pltpu.with_memory_space_constraint(a, pltpu.HBM)
            for a in (slide_lengths, queries, keys, values)
        ],
        [shape(rows, 3 * LANES)] * 2
        + [shape(rows + tile + rows // 2, LANES)] * 2
        + [shape(rows + rows // 2, LANES)] * 2
        + [shape(tile, 4 * LANES)] * 2
        + [shape(mid_rows - tile, 4 * LANES)] * 2
        + [shape(8, LANES, jnp.int32)],
        [
            pltpu.VMEM((group, 3, rows, LANES), BF16),
            pltpu.VMEM((group, 2, rows, rows), BF16),
            pltpu.SMEM(slide_lengths.shape, jnp.int32),
            pltpu.SemaphoreType.DMA((group, 3)),
            pltpu.SemaphoreType.DMA,
        ],
        [hbm] * 4,
    )
    leads, seconds, heads, tails = [packed[n : n + 2] for n in range(0, 8, 2)]
    leads = [exchange(leads[n], "inner", 2 + n) for n in range(2)]
    seconds = [exchange(seconds[n], "inner", 2 + n) for n in range(2)]
    near = exchange(near, "inner", 1)
    other_heads, other_tails = [], []
    for x in range(group, plan.inner, 2):
        for parts, slots in ((heads, other_heads), (tails, other_tails)):
            other = exchange(parts[x >> 1 & 1], "inner", x)
            slots += [other, exchange(other, "inner", 1)]

    top = plan.top_rows
    firsts = [a[:top, LANES : 2 * LANES] for a in (own, near)] + [a[:top] for a in leads]
    lasts = [a[:top, 2 * LANES :] for a in (own, near)] + [
        a[rows : rows + top] for a in leads
    ]
    kv = [jnp.concatenate(slot, axis=1) for slot in zip(firsts, lasts)]
    top_own = jnp.concatenate(kv + [slot[:top] for slot in other_chunks(other_heads)], axis=0)
    tops = [exchange(top_own, "outer", x) for x in range(1, plan.outer)]

    count = group * rows
    scratch = [pltpu.VMEM((count, LANES), BF16)] * 2
    scratch += [pltpu.VMEM((count, 2 * LANES), BF16)]
    scratch += [pltpu.VMEM((group * mid_rows, LANES), BF16)]
    scratch += [pltpu.VMEM((2, 2 * max(mid_rows, rows - mid_rows), count), F32)]
    state = [shape(group * mid_rows, LANES, F32)] * 2 + [shape(group * mid_rows, LANES)]
    rest_one, *state_one = call(
        functools.partial(local_kernel, plan, 0),
        (table, own, near, *leads),
        [shape(group * (rows - mid_rows), LANES, F32), *state],
        scratch,
    )
    local_two = call(
        functools.partial(local_kernel, plan, 1),
        (table, own, near, *seconds, rest_one),
        [shape(rows - mid_rows, LANES)] * group + state,
        scratch,
    )
    rests, state_two = local_two[:group], local_two[group:]
    rests = [rests[0]] + [exchange(rests[x], "inner", x) for x in range(1, group)]
    lead_state = [shape(group * tile, LANES, F32)] * 2 + [shape(group * tile, LANES)]
    n_top = (plan.outer - 1) * plan.inner * plan.top_rows
    n_mid = (plan.inner - group) * mid_rows
    middle = call(
        functools.partial(mid_kernel, plan),
        (
            table,
            *state_one,
            *state_two,
            *other_heads,
            *other_tails,
        ),
        [shape(mid_rows - tile, LANES)] * group + lead_state * 2,
        [pltpu.VMEM((2, n_mid, LANES), BF16)] * 2
        + [pltpu.VMEM((2, (plan.inner - group) * tile, LANES), BF16)]
        + [pltpu.VMEM((2, group * mid_rows, n_mid), F32)],
    )
    middles, lead_state = middle[:group], middle[group:]
    uppers = call(
        functools.partial(top_kernel, plan),
        (table, *lead_state, *middles, *tops),
        [shape(mid_rows, LANES)] * group,
        [pltpu.VMEM((2, n_top, LANES), BF16)] * 2
        + [pltpu.VMEM((2, group * tile, n_top), F32)],
    )
    uppers = [uppers[0]] + [exchange(uppers[x], "inner", x) for x in range(1, group)]
    ordered = call(functools.partial(order_kernel, plan), rests, [shape(rows, HEADS * HEAD_DIM)])[0]
    return call(
        functools.partial(project_kernel, plan),
        (out_weight, ordered, *uppers),
        [shape(rows, out_weight.shape[1])],
        [pltpu.VMEM((rows, HEADS * HEAD_DIM), BF16)],
    )[0]


def solution(mesh):
    tokens = P(("outer", "inner"), None)

    return jax.shard_map(
        shards,
        mesh=mesh,
        in_specs=(tokens, tokens, tokens, P(), P()),
        out_specs=tokens,
        check_vma=False,
    )
```

```python
import functools

import jax
import jax.numpy as jnp
from jax import lax
from jax.experimental import pallas as pl
from jax.experimental.pallas import tpu as pltpu
from jax.sharding import PartitionSpec as P

HEADS = 8
HEAD_DIM = 64
SPARSE = 1024
LANES = 128
FAR = 1 << 30
BARRED = -(2.0**100)
F32 = jnp.float32
BF16 = jnp.bfloat16


def exchange(block, axis, distance):
    count = lax.axis_size(axis)
    return lax.ppermute(block, axis, [(i, i ^ distance) for i in range(count)])


def shift_of(value):
    return value.bit_length() - 1


class Plan:
    def __init__(self, rows, inner, outer):
        self.rows = rows
        self.inner = inner
        self.outer = outer
        self.mid = rows * inner // SPARSE
        self.top = self.mid * outer
        self.group = SPARSE // rows
        self.mid_rows = rows // self.mid
        self.top_rows = rows // self.top
        self.top_tile = max(16, self.top_rows)
        assert self.group == 4 and HEADS == 2 * self.group and 2 * HEAD_DIM == LANES

    def me(self):
        return lax.axis_index("outer") * self.inner + lax.axis_index("inner")

    def pair(self):
        return lax.axis_index("inner") & (self.group - 1)

    def source_row(self, k):
        a = k >> shift_of(self.mid_rows)
        c = (k & (self.mid_rows - 1)) >> shift_of(self.top_rows)
        b = k & (self.top_rows - 1)
        return self.top * b + self.mid * c + a


def dot(a, b, dims):
    return lax.dot_general(a, b, (dims, ((), ())), preferred_element_type=F32)


def pick(wrapped, head, rows):
    return jnp.where(wrapped == ((rows - head) & (rows - 1)), 1.0, 0.0).astype(BF16)


def pack_kernel(plan, lengths_ref, q_ref, k_ref, v_ref, *refs):
    rows, mid_rows, tile = plan.rows, plan.mid_rows, plan.top_tile
    own, near, *outs, table, taken, one_hot, lengths, sems, length_sem = refs
    leads, seconds, heads, tails = [outs[n : n + 2] for n in range(0, 8, 2)]
    copies = []
    for x in (2, 3, 0, 1):
        columns = pl.ds(pl.multiple_of((plan.pair() ^ x) * LANES, LANES), LANES)
        for part, ref in enumerate((q_ref, k_ref, v_ref)):
            copy = pltpu.make_async_copy(ref.at[:, columns], taken.at[x, part], sems.at[x, part])
            copy.start()
            copies.append(copy)
    length_copy = pltpu.make_async_copy(lengths_ref, lengths, length_sem)
    length_copy.start()
    k = lax.broadcasted_iota(jnp.int32, (rows, rows), 0)
    i = lax.broadcasted_iota(jnp.int32, (rows, rows), 1)
    wrapped = (plan.source_row(k) - i) & (rows - 1)
    first = lax.broadcasted_iota(jnp.int32, (rows, LANES), 1) < HEAD_DIM
    for s, x in enumerate((2, 3, 0, 1)):
        for t in range(2):
            one_hot[s, t] = pick(wrapped, 2 * (plan.pair() ^ x) + t, rows)
    for s, x in enumerate((2, 3, 0, 1)):
        if s % 2 == 0:
            for copy in copies[3 * s : 3 * s + 6]:
                copy.wait()
        key, value = taken[x, 1].astype(F32), taken[x, 2].astype(F32)
        value = pltpu.roll(value, HEAD_DIM, axis=1)
        pairs = [jnp.where(first, key, value), jnp.where(first, value, key)]
        blocks = [jnp.concatenate([taken[x, 0], kv.astype(BF16)], axis=1) for kv in pairs]
        one, two = [dot(one_hot[s, t], blocks[t], ((1,), (0,))) for t in range(2)]
        query = jnp.where(first, one[:, :LANES], two[:, :LANES]) * HEAD_DIM**-0.5
        kv_one, kv_two = one[:, LANES:].astype(BF16), two[:, LANES:].astype(BF16)
        if x >= 2:
            low, high = query[: rows // 2], pltpu.roll(query[rows // 2 :], HEAD_DIM, axis=1)
            leads[x - 2][:rows, :] = kv_one
            leads[x - 2][rows + tile :, :] = jnp.where(first[: rows // 2], low, high).astype(BF16)
            leads[x - 2][rows : rows + tile, :] = kv_two[:tile]
            seconds[x - 2][:rows, :] = kv_two
            seconds[x - 2][rows:, :] = jnp.where(first[: rows // 2], high, low).astype(BF16)
        else:
            out = (own, near)[x]
            out[:, :LANES] = query.astype(BF16)
            out[:, LANES : 2 * LANES] = kv_one
            out[:, 2 * LANES :] = kv_two
        at = (x & 1) * 2 * LANES
        for out, low, high in ((heads[x >> 1], 0, tile), (tails[x >> 1], tile, mid_rows)):
            out[:, at : at + LANES] = kv_one[low:high]
            out[:, at + LANES : at + 2 * LANES] = kv_two[low:high]
    length_copy.wait()
    slide_table(lengths, table)


def block_positions(plan, t, rows):
    head = 2 * plan.pair() + t
    return (plan.source_row(row_iota(rows)) + head) & (plan.rows - 1)


def block_inside(plan, table_ref, t, positions, slot):
    base = (plan.me() ^ slot) * plan.rows
    starts = table_ref[2 * t : 2 * t + 1, :] - base
    ends = table_ref[2 * t + 1 : 2 * t + 2, :] - base
    return (positions >= starts) & (positions < ends)


def as_query(block, inside, own):
    return jnp.where(own, block.astype(F32), jnp.where(inside, BARRED, 0.0)).astype(BF16)


def as_key(block, inside, own):
    return jnp.where(own, block.astype(F32), jnp.where(inside, 0.0, 1.0)).astype(BF16)


def as_value(block, own):
    return jnp.where(own, 1.0, block.astype(F32))


def row_iota(count):
    return lax.broadcasted_iota(jnp.int32, (count, LANES), 0)


def share(sums):
    return pltpu.roll(sums, HEAD_DIM, axis=1) / sums


def chunk(refs, x, t, rows):
    ref = refs[x]
    if x < 2:
        return ref[:, :LANES].astype(F32), ref[:, (1 + t) * LANES : (2 + t) * LANES]
    low = ref[ref.shape[0] - rows // 2 :, :].astype(F32)
    return jnp.concatenate([low, pltpu.roll(low, HEAD_DIM, axis=1)], axis=0), ref[:rows, :]


def local_kernel(plan, t, table_ref, *refs):
    rows, group, mid_rows, tile = plan.rows, plan.group, plan.mid_rows, plan.top_tile
    slots, refs = refs[:group], refs[group:]
    if t:
        before, rests, refs = refs[0], refs[1 : 1 + group], refs[1 + group :]
    else:
        rest, refs = refs[0], refs[1:]
    sums_ref, maxima_ref, q_mid, q_s, k_s, v_s, vt_s, s_s = refs
    positions = block_positions(plan, t, rows)
    lane = lax.broadcasted_iota(jnp.int32, (rows, LANES), 1)
    keys = (lane < HEAD_DIM) if t == 0 else (lane >= HEAD_DIM)
    is_top = row_iota(mid_rows) < plan.top_rows
    for x in range(group):
        here = pl.ds(x * rows, rows)
        mid_here = pl.ds(x * mid_rows, mid_rows)
        inside = block_inside(plan, table_ref, t, positions, x)
        query, kv = chunk(slots, x, t, rows)
        kv = kv.astype(F32)
        query = as_query(query, inside, keys)
        q_s[mid_here, :] = query[:mid_rows]
        q_mid[mid_here, :] = query[:mid_rows]
        others = rows - mid_rows
        q_s[pl.ds(group * mid_rows + x * others, others), :] = query[mid_rows:]
        k_s[here, :] = as_key(kv, inside, keys)
        value = as_value(kv, keys)
        low = value.astype(BF16)
        v_s[here, :LANES] = low
        v_s[pl.ds(x * rows, mid_rows), LANES:] = (2.0 * value[:mid_rows]).astype(BF16)
        v_s[pl.ds(x * rows + mid_rows, rows - mid_rows), LANES:] = low[mid_rows:]
        vt_s[mid_here, :] = jnp.where(is_top, value[:mid_rows], 0.0).astype(BF16)
    blocks = [(0, y) for y in range(0, group, 2)] + [(1, y) for y in range(0, group, 2)]
    sizes, first_row = (mid_rows, others), (0, group * mid_rows)

    def score(block):
        kind, y = block
        taken = q_s[pl.ds(first_row[kind] + y * sizes[kind], 2 * sizes[kind]), :]
        return dot(taken, k_s[...], ((1,), (1,)))

    def held(n):
        return s_s.at[n % 2, pl.ds(0, 2 * sizes[blocks[n][0]]), :]

    held(0)[...] = score(blocks[0])
    for n, (kind, y) in enumerate(blocks):
        if n + 1 < len(blocks):
            held(n + 1)[...] = score(blocks[n + 1])
        scores = held(n)[...]
        largest = jnp.max(scores, axis=1, keepdims=True)
        probs = jnp.exp(scores - largest).astype(BF16)
        there = pl.ds(y * sizes[kind], 2 * sizes[kind])
        if kind == 0:
            leads_of = [probs[z * mid_rows : z * mid_rows + tile] for z in range(2)]
            top_probs = jnp.concatenate(leads_of, axis=0)
            top_probs = jnp.concatenate(
                [top_probs[:, z * rows : z * rows + mid_rows] for z in range(group)], axis=1
            )
            sums_ref[there, :] = dot(probs, v_s[:, LANES:], ((1,), (0,)))
            top_sum = dot(top_probs, vt_s[...], ((1,), (0,)))
            for z in range(2):
                sums_ref[pl.ds((y + z) * mid_rows, tile), :] += jnp.where(
                    row_iota(tile) < plan.top_rows, top_sum[z * tile : (z + 1) * tile], 0.0
                )
            maxima_ref[there, :] = jnp.broadcast_to(largest, (2 * mid_rows, LANES))
        else:
            rest_sum = share(dot(probs, v_s[:, :LANES], ((1,), (0,))))
            if t:
                lane = lax.broadcasted_iota(jnp.int32, (2 * others, LANES), 1)
                both = jnp.where(lane < HEAD_DIM, before[there, :], rest_sum).astype(BF16)
                for z in range(2):
                    rests[y + z][...] = both[z * others : (z + 1) * others]
            else:
                rest[there, :] = rest_sum


def other_chunks(arrays):
    width = 2 * LANES
    slots = []
    for n in range(0, len(arrays), 2):
        if isinstance(arrays[n], jax.Array):
            slots += [arrays[n][:, :width], arrays[n + 1][:, width:]]
        else:
            slots += [arrays[n].at[:, :width], arrays[n + 1].at[:, width:]]
    return slots


def mid_kernel(plan, table_ref, *refs):
    group, mid_rows, tile = plan.group, plan.mid_rows, plan.top_tile
    n = plan.inner - group
    states, refs = refs[:6], refs[6:]
    heads, tails, refs = other_chunks(refs[:n]), other_chunks(refs[n : 2 * n]), refs[2 * n :]
    outs, lead_states, (k_s, v_s, vt_s, s_s) = refs[:group], refs[group : group + 6], refs[group + 6 :]
    count = group * mid_rows
    key_lane = lax.broadcasted_iota(jnp.int32, (mid_rows, LANES), 1)
    results = []
    for t in range(2):
        positions = block_positions(plan, t, mid_rows)
        keys = (key_lane < HEAD_DIM) if t == 0 else (key_lane >= HEAD_DIM)
        columns = slice(t * LANES, (t + 1) * LANES)
        for y in range(n):
            inside = block_inside(plan, table_ref, t, positions, group + y)
            parts = (
                (heads[y], 0, tile, y * tile),
                (tails[y], tile, mid_rows, n * tile + y * (mid_rows - tile)),
            )
            for ref, low, high, at in parts:
                kv = ref[:, columns].astype(F32)
                there = pl.ds(at, high - low)
                value = as_value(kv, keys[low:high])
                k_s[t, there, :] = as_key(kv, inside[low:high], keys[low:high])
                v_s[t, there, :] = value.astype(BF16)
                if low == 0:
                    is_top = row_iota(tile) < plan.top_rows
                    vt_s[t, there, :] = jnp.where(is_top, value, 0.0).astype(BF16)
        s_s[t] = dot(states[3 * t + 2][...], k_s[t], ((1,), (1,)))
    for t in range(2):
        old = states[3 * t + 1][...]
        scores = s_s[t]
        new = jnp.maximum(old, jnp.max(scores, axis=1, keepdims=True))
        probs = jnp.exp(scores - new[:, :1]).astype(BF16)
        sums = states[3 * t][...] * jnp.exp(old - new)
        sums = sums + dot(probs, v_s[t], ((1,), (0,)))

        def leading(array):
            return jnp.concatenate(
                [array[x * mid_rows : x * mid_rows + tile] for x in range(group)], axis=0
            )

        extra = dot(leading(probs[:, : n * tile]), vt_s[t], ((1,), (0,)))
        keep = (row_iota(group * tile) & (tile - 1)) < plan.top_rows
        lead_states[3 * t][...] = leading(sums) + jnp.where(keep, extra, 0.0)
        lead_states[3 * t + 1][...] = leading(new)
        lead_states[3 * t + 2][...] = leading(states[3 * t + 2])
        results.append(share(sums))
    lane = lax.broadcasted_iota(jnp.int32, (count, LANES), 1)
    both = jnp.where(lane < HEAD_DIM, results[0], results[1]).astype(BF16)
    for x in range(group):
        outs[x][...] = both[x * mid_rows + tile : (x + 1) * mid_rows]


def top_kernel(plan, table_ref, *refs):
    group, tile = plan.group, plan.top_tile
    states, refs = refs[:6], refs[6:]
    middles, refs = refs[:group], refs[group:]
    tops, refs = refs[: plan.outer - 1], refs[plan.outer - 1 :]
    outs, (k_s, v_s, s_s) = refs[:group], refs[group:]
    count = group * tile
    shift = shift_of(plan.top_rows)
    is_top = (row_iota(count) & (tile - 1)) < plan.top_rows
    n = tops[0].shape[0]
    row = row_iota(n)
    key_lane = lax.broadcasted_iota(jnp.int32, (n, LANES), 1)
    source = plan.me() ^ (row >> shift)
    bases = [(source ^ (e * plan.inner)) * plan.rows for e in range(1, plan.outer)]
    for t in range(2):
        keys = (key_lane < HEAD_DIM) if t == 0 else (key_lane >= HEAD_DIM)
        head = 2 * plan.pair() + t
        offset = (plan.source_row(row & (plan.top_rows - 1)) + head) & (plan.rows - 1)
        starts, ends = table_ref[2 * t : 2 * t + 1, :], table_ref[2 * t + 1 : 2 * t + 2, :]
        for e in range(1, plan.outer):
            kv = tops[e - 1][:, t * LANES : (t + 1) * LANES].astype(F32)
            position = bases[e - 1] + offset
            inside = (position >= starts) & (position < ends)
            there = pl.ds((e - 1) * n, n)
            k_s[t, there, :] = as_key(kv, inside, keys)
            v_s[t, there, :] = as_value(kv, keys).astype(BF16)
        s_s[t] = dot(states[3 * t + 2][...], k_s[t], ((1,), (1,)))
    results = []
    for t in range(2):
        sums, old = states[3 * t][...], states[3 * t + 1][...]
        scores = s_s[t]
        new = jnp.maximum(old, jnp.max(scores, axis=1, keepdims=True))
        probs = jnp.exp(scores - new[:, :1]).astype(BF16)
        merged = sums * jnp.exp(old - new) + dot(probs, v_s[t], ((1,), (0,)))
        results.append(share(jnp.where(is_top, merged, sums)))
    lane = lax.broadcasted_iota(jnp.int32, (count, LANES), 1)
    both = jnp.where(lane < HEAD_DIM, results[0], results[1]).astype(BF16)
    for x in range(group):
        outs[x][:tile] = both[x * tile : (x + 1) * tile]
        outs[x][tile:] = middles[x][...]


def unpermute(plan, parts, low, high, out):
    rows = plan.rows
    i = lax.broadcasted_iota(jnp.int32, (rows, high - low), 0)
    k = lax.broadcasted_iota(jnp.int32, (rows, high - low), 1) + low
    wrapped = (plan.source_row(k) - i) & (rows - 1)
    lane = lax.broadcasted_iota(jnp.int32, (rows, LANES), 1)
    for x in range(plan.group):
        pair = plan.pair() ^ x
        one = dot(pick(wrapped, 2 * pair, rows), parts[x][...], ((1,), (0,)))
        two = dot(pick(wrapped, 2 * pair + 1, rows), parts[x][...], ((1,), (0,)))
        columns = pl.ds(pl.multiple_of(pair * LANES, LANES), LANES)
        value = jnp.where(lane < HEAD_DIM, one, two)
        if low == 0:
            value = value + out[1][:, columns].astype(F32)
        out[0][:, columns] = value.astype(BF16)


def order_kernel(plan, *refs):
    unpermute(plan, refs[:-1], plan.mid_rows, plan.rows, (refs[-1],))


def project_kernel(plan, weight_ref, rest_ref, *refs):
    uppers, (out_ref, flat) = refs[: plan.group], refs[plan.group :]
    unpermute(plan, uppers, 0, plan.mid_rows, (flat, rest_ref))
    out_ref[...] = dot(flat[...], weight_ref[...], ((1,), (0,))).astype(BF16)


def slide_table(lengths_ref, table_ref):
    row = lax.broadcasted_iota(jnp.int32, (8, LANES), 0)
    lane = lax.broadcasted_iota(jnp.int32, (8, LANES), 1)
    slide = lane - jnp.where(row < 2, HEAD_DIM, 0)
    table = jnp.full((8, LANES), FAR, jnp.int32)
    start = jnp.int32(0)
    for s in range(lengths_ref.shape[0]):
        end = start + lengths_ref[s]
        table = jnp.where(slide == s, jnp.where((row & 1) == 1, end, start), table)
        start = end
    table_ref[...] = table


def shape(count, width, kind=BF16):
    return jax.ShapeDtypeStruct((count, width), kind)


def call(kernel, operands, results, scratch=(), in_specs=None):
    vmem = pl.BlockSpec(memory_space=pltpu.VMEM)
    return pl.pallas_call(
        kernel,
        in_specs=in_specs or [vmem] * len(operands),
        out_specs=[vmem] * len(results),
        out_shape=results,
        scratch_shapes=scratch,
        compiler_params=pltpu.CompilerParams(vmem_limit_bytes=24 << 20),
    )(*operands)


def shards(queries, keys, values, out_weight, slide_lengths):
    plan = Plan(queries.shape[0], lax.axis_size("inner"), lax.axis_size("outer"))
    rows, group, mid_rows, tile = plan.rows, plan.group, plan.mid_rows, plan.top_tile
    hbm = pl.BlockSpec(memory_space=pltpu.HBM)
    own, near, *packed, table = call(
        functools.partial(pack_kernel, plan),
        [
            pltpu.with_memory_space_constraint(a, pltpu.HBM)
            for a in (slide_lengths, queries, keys, values)
        ],
        [shape(rows, 3 * LANES)] * 2
        + [shape(rows + tile + rows // 2, LANES)] * 2
        + [shape(rows + rows // 2, LANES)] * 2
        + [shape(tile, 4 * LANES)] * 2
        + [shape(mid_rows - tile, 4 * LANES)] * 2
        + [shape(8, LANES, jnp.int32)],
        [
            pltpu.VMEM((group, 3, rows, LANES), BF16),
            pltpu.VMEM((group, 2, rows, rows), BF16),
            pltpu.SMEM(slide_lengths.shape, jnp.int32),
            pltpu.SemaphoreType.DMA((group, 3)),
            pltpu.SemaphoreType.DMA,
        ],
        [hbm] * 4,
    )
    leads, seconds, heads, tails = [packed[n : n + 2] for n in range(0, 8, 2)]
    leads = [exchange(leads[n], "inner", 2 + n) for n in range(2)]
    seconds = [exchange(seconds[n], "inner", 2 + n) for n in range(2)]
    near = exchange(near, "inner", 1)
    other_heads, other_tails = [], []
    for x in range(group, plan.inner, 2):
        for parts, slots in ((heads, other_heads), (tails, other_tails)):
            other = exchange(parts[x >> 1 & 1], "inner", x)
            slots += [other, exchange(other, "inner", 1)]

    top = plan.top_rows
    firsts = [a[:top, LANES : 2 * LANES] for a in (own, near)] + [a[:top] for a in leads]
    lasts = [a[:top, 2 * LANES :] for a in (own, near)] + [
        a[rows : rows + top] for a in leads
    ]
    kv = [jnp.concatenate(slot, axis=1) for slot in zip(firsts, lasts)]
    top_own = jnp.concatenate(kv + [slot[:top] for slot in other_chunks(other_heads)], axis=0)
    tops = [exchange(top_own, "outer", x) for x in range(1, plan.outer)]

    count = group * rows
    scratch = [pltpu.VMEM((count, LANES), BF16)] * 2
    scratch += [pltpu.VMEM((count, 2 * LANES), BF16)]
    scratch += [pltpu.VMEM((group * mid_rows, LANES), BF16)]
    scratch += [pltpu.VMEM((2, 2 * max(mid_rows, rows - mid_rows), count), F32)]
    state = [shape(group * mid_rows, LANES, F32)] * 2 + [shape(group * mid_rows, LANES)]
    rest_one, *state_one = call(
        functools.partial(local_kernel, plan, 0),
        (table, own, near, *leads),
        [shape(group * (rows - mid_rows), LANES, F32), *state],
        scratch,
    )
    local_two = call(
        functools.partial(local_kernel, plan, 1),
        (table, own, near, *seconds, rest_one),
        [shape(rows - mid_rows, LANES)] * group + state,
        scratch,
    )
    rests, state_two = local_two[:group], local_two[group:]
    rests = [rests[0]] + [exchange(rests[x], "inner", x) for x in range(1, group)]
    lead_state = [shape(group * tile, LANES, F32)] * 2 + [shape(group * tile, LANES)]
    n_top = (plan.outer - 1) * plan.inner * plan.top_rows
    n_mid = (plan.inner - group) * mid_rows
    middle = call(
        functools.partial(mid_kernel, plan),
        (
            table,
            *state_one,
            *state_two,
            *other_heads,
            *other_tails,
        ),
        [shape(mid_rows - tile, LANES)] * group + lead_state * 2,
        [pltpu.VMEM((2, n_mid, LANES), BF16)] * 2
        + [pltpu.VMEM((2, (plan.inner - group) * tile, LANES), BF16)]
        + [pltpu.VMEM((2, group * mid_rows, n_mid), F32)],
    )
    middles, lead_state = middle[:group], middle[group:]
    uppers = call(
        functools.partial(top_kernel, plan),
        (table, *lead_state, *middles, *tops),
        [shape(mid_rows, LANES)] * group,
        [pltpu.VMEM((2, n_top, LANES), BF16)] * 2
        + [pltpu.VMEM((2, group * tile, n_top), F32)],
    )
    uppers = [uppers[0]] + [exchange(uppers[x], "inner", x) for x in range(1, group)]
    ordered = call(functools.partial(order_kernel, plan), rests, [shape(rows, HEADS * HEAD_DIM)])[0]
    return call(
        functools.partial(project_kernel, plan),
        (out_weight, ordered, *uppers),
        [shape(rows, out_weight.shape[1])],
        [pltpu.VMEM((rows, HEADS * HEAD_DIM), BF16)],
    )[0]


def solution(mesh):
    tokens = P(("outer", "inner"), None)

    return jax.shard_map(
        shards,
        mesh=mesh,
        in_specs=(tokens, tokens, tokens, P(), P()),
        out_specs=tokens,
        check_vma=False,
    )
```
